32 devices in a mesh: ap: 8 (over z, y), rg: 4 (over x, core).
Axes of the slice: x: 2, y: 2, z: 4, core: 2. Of those that a mesh axis runs over, the one named last changes fastest.
Arguments:
- raw_echoes: bfloat16 [2, 2048, 4096], P(None, 'ap', 'rg'), may hold values from -6 to 6
- chirp: float32 [2, 128], replicated, may hold values from -0.375 to 0.375
- range_offsets: int32 [8, 2, 4096], P(None, None, 'rg'), may hold values from 0 to 7
- phases: float32 [8, 2, 4096], P(None, None, 'rg'), may hold values from -3.140625 to 3.140625
- tile_table: int32 [64, 16], replicated, may hold values from 0 to 1023, as said below
Outputs:
- image: float32 [2, 2048, 4096], P(None, 'ap', 'rg')
The draws below stay inside these ranges and needn't reach their ends.
Inputs may be any that keep to these rules, and one draw needn't show every extreme that they name: `tile_table`: all entries differ (a permutation of tile indices). The tiles that lie in one device's block of the image (256 pulses by 1024 range bins) go to tiles of distinct devices' blocks, one to each device. The same holds for each set of tiles whose tile rows u share one value of u mod (8) and whose columns lie in one device's range bins.
All inputs are finite; a program needn't handle non-finite values.
Results may differ from the reference program's by a relative error of at most 0.0029.
Values may be sent and summed in bfloat16 or wider, within the bound.
A program may use at most 64 MiB of HBM per device.

```python
import jax
import jax.numpy as jnp
from jax import lax

R = 4096
CHIRP = 128
MERGES = 8
APER = 2048
N_AP = 8
N_RG = 4


def draw_tile_table(key, part):
    row_perm = jax.random.permutation(jax.random.fold_in(key, 11), N_AP).astype(jnp.int32)
    col_perm = jax.random.permutation(jax.random.fold_in(key, 23), N_RG).astype(jnp.int32)
    slot_perm = jax.random.permutation(jax.random.fold_in(key, 37), N_AP).astype(jnp.int32)
    bin_perm = jax.random.permutation(jax.random.fold_in(key, 41), N_RG).astype(jnp.int32)
    shifts = jax.random.randint(jax.random.fold_in(key, 53), (N_AP,), 0, N_RG).astype(jnp.int32)
    source_ap = jnp.arange(N_AP, dtype=jnp.int32)[:, None, None, None]
    inner_row = jnp.arange(N_AP, dtype=jnp.int32)[None, :, None, None]
    source_rg = jnp.arange(N_RG, dtype=jnp.int32)[None, None, :, None]
    inner_col = jnp.arange(N_RG, dtype=jnp.int32)[None, None, None, :]
    target_ap = row_perm[(source_ap + inner_row) % N_AP]
    target_rg = col_perm[(inner_col + source_rg) % N_RG]
    slot_row = slot_perm[source_ap] + 0 * inner_row + 0 * source_rg + 0 * inner_col
    slot_col = bin_perm[(source_rg + shifts[source_ap]) % N_RG] + 0 * inner_row + 0 * inner_col
    tile_row = target_ap * N_AP + slot_row
    tile_col = target_rg * N_RG + slot_col
    destination = tile_row * (N_RG * N_RG) + tile_col
    return destination.reshape(N_AP * N_AP, N_RG * N_RG).astype(jnp.int32)


def with_ends(values, stream_key, least, high):
    place = [jax.random.randint(jax.random.fold_in(stream_key, axis), (), 0, length) for axis, length in enumerate(values.shape)]
    longest = values.shape.index(max(values.shape))
    beside = place[:longest] + [(place[longest] + 1) % values.shape[longest]] + place[longest + 1:]
    return values.at[tuple(place)].set(least).at[tuple(beside)].set(high)


def levels(key, dims, pieces, smallest, high):
    factor_of, own = 1.0, jax.random.fold_in(key, 6)
    for position, shards_of in pieces:
        draws = jnp.exp(jax.random.uniform(jax.random.fold_in(own, position), (shards_of,), jnp.float32, smallest / len(pieces), high / len(pieces)))
        factor_of = factor_of * jnp.repeat(draws, dims[position] // shards_of).reshape([-1 if axis == position else 1 for axis in range(len(dims))])
    return factor_of


def gaussian(own_key, shape, scale, bound, split=(), kind=jnp.bfloat16):
    loudness = levels(own_key, shape, split, -0.22, 0.18) if split else 1.0
    array = jax.random.normal(own_key, shape, jnp.float32) * scale * loudness
    return jnp.minimum(jnp.maximum(array, -bound), bound).astype(kind)


def setup_inputs(seed: int = 0) -> dict:
    key_of = jax.random.split(jax.random.key(seed), 6)
    raw_echoes = gaussian(key_of[0], (2, APER, R), 1.0, 6.0, ((1, 8), (2, 4)))
    chirp = gaussian(key_of[1], (2, CHIRP), (2 * CHIRP) ** -0.5, 0.375, (), jnp.float32)
    range_offsets = with_ends(jax.random.randint(key_of[2], (MERGES, 2, R), 0, 8), jax.random.fold_in(key_of[2], 1), 0, 7).astype(jnp.int32)
    phases = jnp.clip(jax.random.uniform(key_of[3], (MERGES, 2, R), jnp.float32, -3.140625, 3.140625), -3.140625, 3.140625)
    tile_table = draw_tile_table(jax.random.fold_in(key_of[5], 71), 0)
    return dict(raw_echoes=raw_echoes, chirp=chirp, range_offsets=range_offsets, phases=phases, tile_table=tile_table)


root_half = 0.7071067811865476


def toeplitz_table(chirp_taps, window, block):
    tap_count = chirp_taps.shape[1]
    tap_lag = lax.broadcasted_iota(jnp.int32, (window, block), 0) - lax.broadcasted_iota(jnp.int32, (window, block), 1)
    picker = (tap_lag[:, :, None] == lax.broadcasted_iota(jnp.int32, (1, 1, tap_count), 2)).astype(jnp.float32)
    spread = jnp.einsum('wok,ck->cwo', picker, chirp_taps.astype(jnp.float32), precision=lax.Precision.HIGHEST)
    from_real = jnp.stack([spread[0], -spread[1]], axis=1)
    from_imag = jnp.stack([spread[1], spread[0]], axis=1)
    return jnp.stack([from_real, from_imag], axis=0).astype(jnp.bfloat16)


def rotated_term(padded, offsets, angles):
    range_bins = offsets.shape[-1]
    picked = jnp.zeros(padded.shape[:-1] + (range_bins,), jnp.float32)
    for shift_value in range(8):
        picked = jnp.where(offsets == shift_value, padded[..., shift_value:shift_value + range_bins], picked)
    cosine = jnp.cos(angles)
    sine_part = jnp.sin(angles)
    return jnp.stack([picked[0] * cosine - picked[1] * sine_part, picked[0] * sine_part + picked[1] * cosine])


def reference(raw_echoes, chirp, range_offsets, phases, tile_table):
    chirp_taps = chirp.astype(jnp.bfloat16)
    half_taps = CHIRP // 2
    block = min(128, R)
    window = block + CHIRP
    table = toeplitz_table(chirp_taps, window, block).astype(jnp.float32)
    padded = jnp.pad(raw_echoes, ((0, 0), (0, 0), (half_taps, half_taps)))

    def one_block(index):
        piece = lax.dynamic_slice_in_dim(padded, index * block, window, 2).astype(jnp.float32)
        return jnp.einsum('cpw,cwdo->dpo', piece, table, precision=lax.Precision.HIGHEST)

    filtered = lax.map(one_block, jnp.arange(R // block, dtype=jnp.int32))
    field = filtered.transpose(1, 2, 0, 3).reshape(2, APER, R)
    for merge_level in range(MERGES):
        distance = APER // 2 ** MERGES * 2 ** merge_level
        padded_field = jnp.pad(field, ((0, 0), (0, 0), (4, 4)))
        grouped = padded_field.reshape(2, APER // (2 * distance), 2, distance, R + 8)
        lower_term = rotated_term(grouped[:, :, 0], range_offsets[merge_level, 0], phases[merge_level, 0])
        upper_term = rotated_term(grouped[:, :, 1], range_offsets[merge_level, 1], phases[merge_level, 1])
        merged = jnp.stack([lower_term + upper_term, lower_term - upper_term], axis=2) * root_half
        field = merged.reshape(2, APER, R)
    tile_rows = APER // (N_AP * N_AP)
    tile_bins = R // (N_RG * N_RG)
    row_tiles = N_AP * N_AP
    col_tiles = N_RG * N_RG
    tiles = field.reshape(2, row_tiles, tile_rows, col_tiles, tile_bins).transpose(0, 1, 3, 2, 4)
    tiles = tiles.reshape(2, row_tiles * col_tiles, tile_rows, tile_bins)
    flat_table = tile_table.reshape(-1).astype(jnp.int32)
    inverse = jnp.zeros_like(flat_table).at[flat_table].set(jnp.arange(row_tiles * col_tiles, dtype=jnp.int32))
    placed = jnp.take(tiles, inverse, axis=1)
    placed = placed.reshape(2, row_tiles, col_tiles, tile_rows, tile_bins).transpose(0, 1, 3, 2, 4)
    return placed.reshape(2, APER, R)
```

```python
import functools

import jax
import jax.numpy as jnp
from jax import lax
from jax.experimental import pallas as pl
from jax.experimental.pallas import tpu as pltpu
from jax.sharding import PartitionSpec as P

root_half = 0.7071067811865476
LANES = 128
MESH = pl.DeviceIdType.MESH


def hadamard(values):
    values = list(values)
    step = 1
    while step < len(values):
        for i in range(len(values)):
            if not i & step:
                a, b = values[i], values[i + step]
                values[i], values[i + step] = a + b, a - b
        step *= 2
    return values


def cos_sin(angle):
    turns = jnp.floor(angle * 0.6366197723675814 + 0.5)
    y = angle - turns * 1.5703125
    y = y - turns * 4.837512969970703e-4
    y = y - turns * 7.549789948768648e-8
    z = y * y
    sine = y * (1.0 + z * (-1 / 6 + z * (1 / 120 + z * (-1 / 5040 + z * (1 / 362880)))))
    cosine = 1.0 + z * (-0.5 + z * (1 / 24 + z * (-1 / 720 + z * (1 / 40320))))
    quarter = turns.astype(jnp.int32)
    odd = (quarter & 1) == 1
    c = jnp.where(odd, sine, cosine)
    s = jnp.where(odd, cosine, sine)
    c = jnp.where(((quarter + 1) & 2) == 2, -c, c)
    s = jnp.where((quarter & 2) == 2, -s, s)
    return c, s


def lane_pick(low, high, spot, in_low):
    return jnp.where(
        in_low,
        jnp.take_along_axis(low, spot, axis=1),
        jnp.take_along_axis(high, spot, axis=1),
    )


def filter_table(taps_ref):
    def spread(row):
        padded = jnp.concatenate([row, jnp.zeros_like(row)], axis=1)
        padded = jnp.broadcast_to(padded, (LANES, 2 * LANES))
        return pltpu.roll(padded, 0, 1, stride=1, stride_axis=0)

    real, imag = spread(taps_ref[0:1, :]), spread(taps_ref[1:2, :])
    return jnp.concatenate(
        [jnp.concatenate([real, imag], axis=1), jnp.concatenate([-imag, real], axis=1)], axis=0
    ).astype(jnp.bfloat16)


def image_kernel(
    levels,
    ap_count,
    rg_count,
    taps_hbm,
    raw_hbm,
    offsets_hbm,
    phases_hbm,
    tile_table_hbm,
    placed,
    taps,
    raw,
    offsets,
    phases,
    tile_table,
    raw_edges,
    offset_edges,
    phase_edges,
    table,
    ext,
    spots,
    cosines,
    sines,
    terms,
    first_out,
    first_in,
    tiles,
    second_out,
    landed_real,
    landed_imag,
    routes_line,
    routes,
    halo_send,
    halo_recv,
    first_send,
    first_recv,
    second_send,
    second_recv,
    routes_sem,
    load_sem,
):
    ap_here, rg_here = lax.axis_index("ap"), lax.axis_index("rg")
    devices = ap_count * rg_count
    here_id = ap_here * rg_count + rg_here
    pulses, range_bins = raw.shape[1], raw.shape[2]
    tile_rows, tile_bins = first_out.shape[3], first_out.shape[4]
    chunks = first_out.shape[2]
    distance = pulses * ap_count // 2**levels
    leaves = pulses // distance
    blocks = range_bins // LANES
    per_chunk = tile_bins // LANES
    first_bin = rg_here * range_bins
    total_bins = rg_count * range_bins
    rows_of = 2 * levels

    loads = [
        pltpu.make_async_copy(source, target, load_sem.at[n])
        for n, (source, target) in enumerate(
            (
                (offsets_hbm, offsets),
                (phases_hbm, phases),
                (taps_hbm, taps),
                (raw_hbm, raw),
                (tile_table_hbm, tile_table),
            )
        )
    ]
    for load in loads:
        load.start()
    landed = (landed_real, landed_imag)
    barrier = pltpu.get_barrier_semaphore()

    @pl.loop(1, devices)
    def _(step):
        peer = lax.rem(here_id + step, devices)
        pl.semaphore_signal(
            barrier, inc=1, device_id=(peer // rg_count, lax.rem(peer, rg_count)), device_id_type=MESH
        )

    for load in loads:
        load.wait()
    weights = filter_table(taps)

    def raw_segment(part, k):
        if k == 0:
            return raw_edges[0, part]
        if k == blocks + 1:
            return raw_edges[1, part]
        return raw[part, :, (k - 1) * LANES : k * LANES]

    def filtered(k):
        window = jnp.concatenate(
            [raw_segment(0, k), raw_segment(0, k + 1), raw_segment(1, k), raw_segment(1, k + 1)], axis=1
        )
        both = lax.dot_general(
            window, weights, (((1,), (1,)), ((), ())), preferred_element_type=jnp.float32
        )
        ext[0, :, k * LANES : (k + 1) * LANES] = both[:, :LANES]
        ext[1, :, k * LANES : (k + 1) * LANES] = both[:, LANES:]

    def tabled(k):
        first_half = lax.broadcasted_iota(jnp.int32, (rows_of, LANES), 1) < LANES // 2
        for kind, (middle, edges) in enumerate(((offsets, offset_edges), (phases, phase_edges))):

            def segment(k):
                if k == 0:
                    piece = [edges[0, level] for level in range(levels)]
                elif k == blocks + 1:
                    piece = [edges[1, level] for level in range(levels)]
                else:
                    columns = slice((k - 1) * LANES, k * LANES)
                    piece = [middle[level, :, columns] for level in range(levels)]
                piece = jnp.concatenate([part.astype(jnp.float32) for part in piece], axis=0)
                return pltpu.roll(piece, LANES // 2, 1)

            table[kind * rows_of : (kind + 1) * rows_of, k * LANES : (k + 1) * LANES] = jnp.where(
                first_half, segment(k), segment(k + 1)
            )


    def halo_copies(side):
        columns = pl.ds(0, LANES) if side == 0 else pl.ds(range_bins - LANES, LANES)
        to = (ap_here, rg_here - 1 if side == 0 else rg_here + 1)
        pairs = (
            (raw.at[:, :, columns], raw_edges.at[1 - side]),
            (offsets.at[:, :, columns], offset_edges.at[1 - side]),
            (phases.at[:, :, columns], phase_edges.at[1 - side]),
        )
        return [
            pltpu.make_async_remote_copy(
                src_ref=source,
                dst_ref=target,
                send_sem=halo_send.at[side, n],
                recv_sem=halo_recv.at[1 - side, n],
                device_id=to,
                device_id_type=MESH,
            )
            for n, (source, target) in enumerate(pairs)
        ]

    has = (rg_here > 0, rg_here < rg_count - 1)

    leaf = lax.broadcasted_iota(jnp.int32, (leaves, LANES), 0) + ap_here * leaves
    lane = lax.broadcasted_iota(jnp.int32, (leaves, LANES), 1)
    radix = min(8, leaves)
    groups = leaves // radix

    def block(chunk, half):
        k = chunk * per_chunk + half
        here = pl.multiple_of(k * LANES, LANES)
        after = pl.multiple_of(k * LANES + LANES, LANES)
        inside = pl.multiple_of(half * LANES, LANES)
        origin = first_bin + k * LANES - LANES // 2
        rel = lane + LANES // 2
        angle = jnp.zeros((leaves, LANES), jnp.float32)
        valid = jnp.ones((leaves, LANES), jnp.bool_)
        for level in reversed(range(levels)):
            upper = ((leaf >> level) & 1) == 1
            in_low = rel < LANES
            spot = rel & (LANES - 1)

            def looked_up(kind):
                row = kind * rows_of + level * 2
                pair = [
                    jnp.where(
                        upper,
                        table[row + 1 : row + 2, pl.ds(at, LANES)],
                        table[row : row + 1, pl.ds(at, LANES)],
                    )
                    for at in (here, after)
                ]
                return lane_pick(pair[0], pair[1], spot, in_low)

            offset = looked_up(0).astype(jnp.int32)
            angle = angle + looked_up(1)
            rel = rel + offset - 4
            where_now = rel + origin
            valid = valid & (where_now >= 0) & (where_now < total_bins)
        c, s = cos_sin(angle)
        spots[...] = rel
        cosines[...] = jnp.where(valid, c, 0.0)
        sines[...] = jnp.where(valid, s, 0.0)
        for group in range(groups):
            reals, imags = [], []
            for member in range(radix):
                one = group * radix + member
                rows = slice(one * distance, (one + 1) * distance)
                shape = (distance, LANES)
                at = jnp.broadcast_to(spots[one : one + 1, :], shape)
                cosine = jnp.broadcast_to(cosines[one : one + 1, :], shape)
                sine = jnp.broadcast_to(sines[one : one + 1, :], shape)
                in_low = at < LANES
                spot = at & (LANES - 1)
                real = lane_pick(
                    ext[0, rows, pl.ds(here, LANES)], ext[0, rows, pl.ds(after, LANES)], spot, in_low
                )
                imag = lane_pick(
                    ext[1, rows, pl.ds(here, LANES)], ext[1, rows, pl.ds(after, LANES)], spot, in_low
                )
                reals.append(real * cosine - imag * sine)
                imags.append(real * sine + imag * cosine)
            for part, values in enumerate((hadamard(reals), hadamard(imags))):
                for member, value in enumerate(values):
                    one = group * radix + member
                    terms[part, one * distance : (one + 1) * distance, :] = value
        span = radix * distance
        piece = min(tile_rows, span)
        for part in range(2):
            for begin in range(0, span, piece):
                sums = hadamard(
                    [terms[part, g * span + begin : g * span + begin + piece, :] for g in range(groups)]
                )
                for g, value in enumerate(sums):
                    row = g * span + begin
                    low = row % tile_rows
                    first_out[
                        part, row // tile_rows, chunk, low : low + piece, pl.ds(inside, LANES)
                    ] = value.astype(jnp.bfloat16)

    def send_first(part, chunk):
        @pl.loop(1, ap_count)
        def _(step):
            peer = lax.rem(ap_here + step, ap_count)
            pltpu.make_async_remote_copy(
                src_ref=first_out.at[part, peer, chunk],
                dst_ref=first_in.at[part, ap_here, chunk],
                send_sem=first_send.at[part],
                recv_sem=first_recv.at[part],
                device_id=(peer, rg_here),
                device_id_type=MESH,
            ).start()

    def run_chunk(chunk):
        @pl.loop(0, per_chunk)
        def _(half):
            block(chunk, half)

    ahead = range(per_chunk, 2 * per_chunk + 1) if chunks > 2 else range(0)
    for k in ahead:
        filtered(k)
        tabled(k)
    if chunks > 2:
        run_chunk(1)
    pl.semaphore_wait(barrier, devices - 1)
    if chunks > 2:
        send_first(0, 1)
        send_first(1, 1)
    for side in range(2):

        @pl.when(has[side])
        def _():
            for copy in halo_copies(side):
                copy.start()

        @pl.when(jnp.logical_not(has[side]))
        def _():
            raw_edges[side] = jnp.zeros(raw_edges.shape[1:], raw_edges.dtype)
            offset_edges[side] = jnp.zeros(offset_edges.shape[1:], offset_edges.dtype)
            phase_edges[side] = jnp.zeros(phase_edges.shape[1:], phase_edges.dtype)

    for k in range(1, blocks):
        if k not in ahead:
            filtered(k)
            tabled(k)

    def run_and_send(chunk):
        run_chunk(chunk)
        send_first(0, chunk)

    if chunks > 3:
        pl.loop(2, chunks - 1)(run_and_send)

    for side in range(2):

        @pl.when(has[side])
        def _():
            for copy in halo_copies(1 - side):
                copy.wait_recv()

    for k in (0, blocks):
        filtered(k)
        tabled(k)

    pl.loop(0, min(chunks, 2))(lambda i: run_and_send(i * (chunks - 1)))
    send_first(1, 0)
    if chunks > 1:
        pl.loop(2 if chunks > 2 else 1, chunks)(lambda i: send_first(1, i))

    columns_all, lines = tile_table.shape
    shape = (devices, lines)
    row_id = lax.broadcasted_iota(jnp.int32, shape, 0)
    line_id = lax.broadcasted_iota(jnp.int32, shape, 1)
    slot_here = (ap_here * ap_count + row_id // rg_count) * columns_all + rg_here * rg_count
    slot_here = slot_here + row_id % rg_count
    order_now = jnp.zeros(shape, jnp.int32)
    source_now = jnp.zeros(shape, jnp.int32)
    for v in range(columns_all):
        slot = tile_table[v : v + 1, :]
        target = slot // columns_all // ap_count * rg_count + slot % columns_all // rg_count
        slot, target = jnp.broadcast_to(slot, shape), jnp.broadcast_to(target, shape)
        holder = line_id % ap_count * rg_count + v // rg_count
        source_now = source_now + jnp.where(slot == slot_here, holder, 0)
        mine = (target == row_id) & (holder == here_id)
        order_now = order_now + jnp.where(mine, line_id // ap_count * rg_count + v % rg_count, 0)
    diagonal = lax.broadcasted_iota(jnp.int32, (devices, LANES), 0) == lax.broadcasted_iota(
        jnp.int32, (devices, LANES), 1
    )
    for n, found in enumerate((order_now, source_now)):
        column = jnp.minimum(jnp.sum(found, axis=1, keepdims=True), devices - 1)
        column = jnp.where(diagonal, jnp.broadcast_to(column, (devices, LANES)), 0)
        routes_line[n : n + 1, :] = jnp.sum(column, axis=0, keepdims=True)
    routes_copy = pltpu.make_async_copy(routes_line, routes, routes_sem)
    routes_copy.start()
    routes_copy.wait()

    for side in range(2):

        @pl.when(has[side])
        def _():
            for copy in halo_copies(side):
                copy.wait_send()

    scale = root_half**levels

    def first_all(part):
        return pltpu.make_async_remote_copy(
            src_ref=first_out.at[part, pl.ds(0, ap_count - 1)],
            dst_ref=first_in.at[part, pl.ds(0, ap_count - 1)],
            send_sem=first_send.at[part],
            recv_sem=first_recv.at[part],
            device_id=(lax.rem(ap_here + 1, ap_count), rg_here),
            device_id_type=MESH,
        )

    def second_all(part):
        return pltpu.make_async_remote_copy(
            src_ref=second_out.at[part, pl.ds(0, devices - 1)],
            dst_ref=landed[part].at[pl.ds(0, devices - 1)],
            send_sem=second_send.at[part],
            recv_sem=second_recv.at[part],
            device_id=(lax.rem(ap_here + 1, ap_count), rg_here),
            device_id_type=MESH,
        )

    for part in range(2):
        first_in[part, ap_here] = first_out[part, ap_here]
        first_all(part).wait_recv()
        for column in range(chunks):
            for at in range(0, tile_bins, LANES):
                sums = hadamard(
                    [
                        first_in[part, s, column, :, at : at + LANES].astype(jnp.float32)
                        for s in range(ap_count)
                    ]
                )
                for o, value in enumerate(sums):
                    tiles[o * chunks + column, :, at : at + LANES] = (value * scale).astype(
                        jnp.bfloat16
                    )

        @pl.loop(0, devices)
        def _(d):
            second_out[part, d] = tiles[routes[0, d]]

        landed[part][here_id] = second_out[part, here_id]

        @pl.loop(1, devices)
        def _(step):
            peer = lax.rem(here_id + step, devices)
            pltpu.make_async_remote_copy(
                src_ref=second_out.at[part, peer],
                dst_ref=landed[part].at[here_id],
                send_sem=second_send.at[part],
                recv_sem=second_recv.at[part],
                device_id=(peer // rg_count, lax.rem(peer, rg_count)),
                device_id_type=MESH,
            ).start()

    for part in range(2):
        second_all(part).wait_recv()
        for i in range(ap_count):
            for j in range(chunks):
                placed[
                    part, i * tile_rows : (i + 1) * tile_rows, j * tile_bins : (j + 1) * tile_bins
                ] = landed[part][routes[1, i * chunks + j]].astype(jnp.float32)
    for part in range(2):
        first_all(part).wait_send()
        second_all(part).wait_send()


def per_device(raw_echoes, chirp, range_offsets, phases, tile_table):
    ap_count, rg_count = lax.axis_size("ap"), lax.axis_size("rg")
    devices = ap_count * rg_count
    levels = range_offsets.shape[0]
    _, pulses, range_bins = raw_echoes.shape
    distance = pulses * ap_count // 2**levels
    leaves = pulses // distance
    tile_rows = pulses // ap_count
    tile_bins = range_bins // rg_count

    placed = pl.pallas_call(
        functools.partial(image_kernel, levels, ap_count, rg_count),
        out_shape=pltpu.VMEM((2, pulses, range_bins), jnp.float32),
        in_specs=[pl.BlockSpec(memory_space=pltpu.HBM)] * 5,
        out_specs=pl.BlockSpec(memory_space=pltpu.VMEM),
        scratch_shapes=[
            pltpu.VMEM(chirp.shape, chirp.dtype),
            pltpu.VMEM(raw_echoes.shape, raw_echoes.dtype),
            pltpu.VMEM(range_offsets.shape, range_offsets.dtype),
            pltpu.VMEM(phases.shape, phases.dtype),
            pltpu.VMEM(tile_table.shape[::-1], tile_table.dtype),
            pltpu.VMEM((2, 2, pulses, LANES), jnp.bfloat16),
            pltpu.VMEM((2, levels, 2, LANES), jnp.int32),
            pltpu.VMEM((2, levels, 2, LANES), jnp.float32),
            pltpu.VMEM((4 * levels, range_bins + LANES), jnp.float32),
            pltpu.VMEM((2, pulses, range_bins + LANES), jnp.float32),
            pltpu.VMEM((leaves, LANES), jnp.int32),
            pltpu.VMEM((leaves, LANES), jnp.float32),
            pltpu.VMEM((leaves, LANES), jnp.float32),
            pltpu.VMEM((2, pulses, LANES), jnp.float32),
            pltpu.VMEM((2, ap_count, rg_count, tile_rows, tile_bins), jnp.bfloat16),
            pltpu.VMEM((2, ap_count, rg_count, tile_rows, tile_bins), jnp.bfloat16),
            pltpu.VMEM((devices, tile_rows, tile_bins), jnp.bfloat16),
            pltpu.VMEM((2, devices, tile_rows, tile_bins), jnp.bfloat16),
            pltpu.VMEM((devices, tile_rows, tile_bins), jnp.bfloat16),
            pltpu.VMEM((devices, tile_rows, tile_bins), jnp.bfloat16),
            pltpu.VMEM((2, LANES), jnp.int32),
            pltpu.SMEM((2, LANES), jnp.int32),
            pltpu.SemaphoreType.DMA((2, 3)),
            pltpu.SemaphoreType.DMA((2, 3)),
            pltpu.SemaphoreType.DMA((2,)),
            pltpu.SemaphoreType.DMA((2,)),
            pltpu.SemaphoreType.DMA((2,)),
            pltpu.SemaphoreType.DMA((2,)),
            pltpu.SemaphoreType.DMA,
            pltpu.SemaphoreType.DMA((5,)),
        ],
        compiler_params=pltpu.CompilerParams(collective_id=0, has_side_effects=True, vmem_limit_bytes=24 * 2**20),
    )(
        *(
            pltpu.with_memory_space_constraint(operand, pltpu.HBM)
            for operand in (chirp, raw_echoes, range_offsets, phases, tile_table.T)
        )
    )
    return placed


def solution(mesh):
    placed = (P(None, "ap", "rg"), P(), P(None, None, "rg"), P(None, None, "rg"), P())
    return jax.shard_map(
        per_device, mesh=mesh, in_specs=placed, out_specs=P(None, "ap", "rg"), check_vma=False
    )
```

```python
import functools

import jax
import jax.numpy as jnp
from jax import lax
from jax.experimental import pallas as pl
from jax.experimental.pallas import tpu as pltpu
from jax.sharding import PartitionSpec as P

root_half = 0.7071067811865476
LANES = 128
MESH = pl.DeviceIdType.MESH


def hadamard(values):
    values = list(values)
    step = 1
    while step < len(values):
        for i in range(len(values)):
            if not i & step:
                a, b = values[i], values[i + step]
                values[i], values[i + step] = a + b, a - b
        step *= 2
    return values


def cos_sin(angle):
    turns = jnp.floor(angle * 0.6366197723675814 + 0.5)
    y = angle - turns * 1.5703125
    y = y - turns * 4.837512969970703e-4
    y = y - turns * 7.549789948768648e-8
    z = y * y
    sine = y * (1.0 + z * (-1 / 6 + z * (1 / 120 + z * (-1 / 5040 + z * (1 / 362880)))))
    cosine = 1.0 + z * (-0.5 + z * (1 / 24 + z * (-1 / 720 + z * (1 / 40320))))
    quarter = turns.astype(jnp.int32)
    odd = (quarter & 1) == 1
    c = jnp.where(odd, sine, cosine)
    s = jnp.where(odd, cosine, sine)
    c = jnp.where(((quarter + 1) & 2) == 2, -c, c)
    s = jnp.where((quarter & 2) == 2, -s, s)
    return c, s


def lane_pick(low, high, spot, in_low):
    return jnp.where(
        in_low,
        jnp.take_along_axis(low, spot, axis=1),
        jnp.take_along_axis(high, spot, axis=1),
    )


def filter_table(taps_ref):
    def spread(row):
        padded = jnp.concatenate([row, jnp.zeros_like(row)], axis=1)
        padded = jnp.broadcast_to(padded, (LANES, 2 * LANES))
        return pltpu.roll(padded, 0, 1, stride=1, stride_axis=0)

    real, imag = spread(taps_ref[0:1, :]), spread(taps_ref[1:2, :])
    return jnp.concatenate(
        [jnp.concatenate([real, imag], axis=1), jnp.concatenate([-imag, real], axis=1)], axis=0
    ).astype(jnp.bfloat16)


def image_kernel(
    levels,
    ap_count,
    rg_count,
    taps_hbm,
    raw_hbm,
    offsets_hbm,
    phases_hbm,
    tile_table_hbm,
    placed,
    taps,
    raw,
    offsets,
    phases,
    tile_table,
    raw_edges,
    offset_edges,
    phase_edges,
    weights,
    table,
    ext,
    spots,
    cosines,
    sines,
    terms,
    first_out,
    first_in,
    tiles,
    second_out,
    landed_real,
    landed_imag,
    routes_line,
    routes,
    halo_send,
    halo_recv,
    first_send,
    first_recv,
    second_send,
    second_recv,
    routes_sem,
    load_sem,
):
    ap_here, rg_here = lax.axis_index("ap"), lax.axis_index("rg")
    devices = ap_count * rg_count
    here_id = ap_here * rg_count + rg_here
    pulses, range_bins = raw.shape[1], raw.shape[2]
    tile_rows, tile_bins = tiles.shape[1], tiles.shape[2]
    chunks = range_bins // tile_bins
    distance = pulses * ap_count // 2**levels
    leaves = pulses // distance
    blocks = range_bins // LANES
    per_chunk = tile_bins // LANES
    first_bin = rg_here * range_bins
    total_bins = rg_count * range_bins
    rows_of = 2 * levels

    loads = [
        pltpu.make_async_copy(source, target, load_sem.at[n])
        for n, (source, target) in enumerate(
            (
                (taps_hbm, taps),
                (raw_hbm, raw),
                (offsets_hbm, offsets),
                (phases_hbm, phases),
                (tile_table_hbm, tile_table),
            )
        )
    ]
    for load in loads:
        load.start()
    landed = (landed_real, landed_imag)
    barrier = pltpu.get_barrier_semaphore()

    @pl.loop(1, ap_count)
    def _(step):
        pl.semaphore_signal(
            barrier, inc=1, device_id=(lax.rem(ap_here + step, ap_count), rg_here), device_id_type=MESH
        )

    @pl.loop(1, rg_count)
    def _(step):
        pl.semaphore_signal(
            barrier, inc=1, device_id=(ap_here, lax.rem(rg_here + step, rg_count)), device_id_type=MESH
        )

    loads[0].wait()
    weights[...] = filter_table(taps)
    for load in loads[1:]:
        load.wait()

    def columns_of(k):
        return pl.ds(pl.multiple_of(k * LANES, LANES), LANES)

    def raw_segment(part, k):
        if isinstance(k, int) and k == 0:
            return raw_edges[0, part]
        if isinstance(k, int) and k == blocks + 1:
            return raw_edges[1, part]
        return raw[part, :, columns_of(k - 1)]

    def filtered(k):
        window = jnp.concatenate(
            [raw_segment(0, k), raw_segment(0, k + 1), raw_segment(1, k), raw_segment(1, k + 1)], axis=1
        )
        both = lax.dot_general(
            window, weights[...], (((1,), (1,)), ((), ())), preferred_element_type=jnp.float32
        )
        ext[0, :, columns_of(k)] = both[:, :LANES]
        ext[1, :, columns_of(k)] = both[:, LANES:]

    def tabled(k):
        first_half = lax.broadcasted_iota(jnp.int32, (rows_of, LANES), 1) < LANES // 2
        for kind, (middle, edges) in enumerate(((offsets, offset_edges), (phases, phase_edges))):

            def segment(k):
                if isinstance(k, int) and k == 0:
                    piece = [edges[0, level] for level in range(levels)]
                elif isinstance(k, int) and k == blocks + 1:
                    piece = [edges[1, level] for level in range(levels)]
                else:
                    piece = [middle[level, :, columns_of(k - 1)] for level in range(levels)]
                piece = jnp.concatenate([part.astype(jnp.float32) for part in piece], axis=0)
                return pltpu.roll(piece, LANES // 2, 1)

            table[kind * rows_of : (kind + 1) * rows_of, columns_of(k)] = jnp.where(
                first_half, segment(k), segment(k + 1)
            )

    def halo_copies(side):
        columns = pl.ds(0, LANES) if side == 0 else pl.ds(range_bins - LANES, LANES)
        to = (ap_here, rg_here - 1 if side == 0 else rg_here + 1)
        pairs = (
            (raw.at[:, :, columns], raw_edges.at[1 - side]),
            (offsets.at[:, :, columns], offset_edges.at[1 - side]),
            (phases.at[:, :, columns], phase_edges.at[1 - side]),
        )
        return [
            pltpu.make_async_remote_copy(
                src_ref=source,
                dst_ref=target,
                send_sem=halo_send.at[side, n],
                recv_sem=halo_recv.at[1 - side, n],
                device_id=to,
                device_id_type=MESH,
            )
            for n, (source, target) in enumerate(pairs)
        ]

    has = (rg_here > 0, rg_here < rg_count - 1)

    leaf = lax.broadcasted_iota(jnp.int32, (leaves, LANES), 0) + ap_here * leaves
    lane = lax.broadcasted_iota(jnp.int32, (leaves, LANES), 1)
    radix = min(8, leaves)
    groups = leaves // radix

    def block(k):
        here = pl.multiple_of(k * LANES, LANES)
        after = pl.multiple_of(k * LANES + LANES, LANES)
        origin = first_bin + k * LANES - LANES // 2
        rel = lane + LANES // 2
        angle = jnp.zeros((leaves, LANES), jnp.float32)
        valid = jnp.ones((leaves, LANES), jnp.bool_)
        for level in reversed(range(levels)):
            upper = ((leaf >> level) & 1) == 1
            in_low = rel < LANES
            spot = rel & (LANES - 1)

            def looked_up(kind):
                row = kind * rows_of + level * 2
                pair = [
                    jnp.where(
                        upper,
                        table[row + 1 : row + 2, pl.ds(at, LANES)],
                        table[row : row + 1, pl.ds(at, LANES)],
                    )
                    for at in (here, after)
                ]
                return lane_pick(pair[0], pair[1], spot, in_low)

            offset = looked_up(0).astype(jnp.int32)
            angle = angle + looked_up(1)
            rel = rel + offset - 4
            where_now = rel + origin
            valid = valid & (where_now >= 0) & (where_now < total_bins)
        c, s = cos_sin(angle)
        spots[...] = rel
        cosines[...] = jnp.where(valid, c, 0.0)
        sines[...] = jnp.where(valid, s, 0.0)
        for group in range(groups):
            reals, imags = [], []
            for member in range(radix):
                one = group * radix + member
                rows = slice(one * distance, (one + 1) * distance)
                shape = (distance, LANES)
                at = jnp.broadcast_to(spots[one : one + 1, :], shape)
                cosine = jnp.broadcast_to(cosines[one : one + 1, :], shape)
                sine = jnp.broadcast_to(sines[one : one + 1, :], shape)
                in_low = at < LANES
                spot = at & (LANES - 1)
                real = lane_pick(
                    ext[0, rows, pl.ds(here, LANES)], ext[0, rows, pl.ds(after, LANES)], spot, in_low
                )
                imag = lane_pick(
                    ext[1, rows, pl.ds(here, LANES)], ext[1, rows, pl.ds(after, LANES)], spot, in_low
                )
                reals.append(real * cosine - imag * sine)
                imags.append(real * sine + imag * cosine)
            for part, values in enumerate((hadamard(reals), hadamard(imags))):
                for member, value in enumerate(values):
                    one = group * radix + member
                    terms[part, one * distance : (one + 1) * distance, :] = value
        span = radix * distance
        piece = min(tile_rows, span)
        for part in range(2):
            for begin in range(0, span, piece):
                sums = hadamard(
                    [terms[part, g * span + begin : g * span + begin + piece, :] for g in range(groups)]
                )
                for g, value in enumerate(sums):
                    row = g * span + begin
                    low = row % tile_rows
                    first_out[part, row // tile_rows, k, low : low + piece, :] = value.astype(
                        jnp.bfloat16
                    )

    def send_first(part, k):
        @pl.loop(1, ap_count)
        def _(step):
            peer = lax.rem(ap_here + step, ap_count)
            pltpu.make_async_remote_copy(
                src_ref=first_out.at[part, peer, k],
                dst_ref=first_in.at[part, ap_here, k],
                send_sem=first_send.at[part],
                recv_sem=first_recv.at[part],
                device_id=(peer, rg_here),
                device_id_type=MESH,
            ).start()

    def open_edges():
        pl.semaphore_wait(barrier, ap_count + rg_count - 2)
        for side in range(2):

            @pl.when(has[side])
            def _():
                for copy in halo_copies(side):
                    copy.start()

            @pl.when(jnp.logical_not(has[side]))
            def _():
                raw_edges[side] = jnp.zeros(raw_edges.shape[1:], raw_edges.dtype)
                offset_edges[side] = jnp.zeros(offset_edges.shape[1:], offset_edges.dtype)
                phase_edges[side] = jnp.zeros(phase_edges.shape[1:], phase_edges.dtype)

    if blocks > 2:
        filtered(1)
        tabled(1)

        @pl.loop(1, blocks - 1)
        def _(k):
            filtered(k + 1)
            tabled(k + 1)
            block(k)
            pl.when(k == 1)(open_edges)
            send_first(0, k)
    else:
        open_edges()
        for k in range(1, blocks):
            filtered(k)
            tabled(k)

    for side in range(2):

        @pl.when(has[side])
        def _():
            for copy in halo_copies(1 - side):
                copy.wait_recv()

    for k in (0, blocks):
        filtered(k)
        tabled(k)

    @pl.loop(0, min(blocks, 2))
    def _(i):
        block(i * (blocks - 1))
        send_first(0, i * (blocks - 1))

    pl.loop(0, blocks)(lambda k: send_first(1, k))

    columns_all, lines = tile_table.shape
    shape = (devices, lines)
    row_id = lax.broadcasted_iota(jnp.int32, shape, 0)
    line_id = lax.broadcasted_iota(jnp.int32, shape, 1)
    slot_here = (ap_here * ap_count + row_id // rg_count) * columns_all + rg_here * rg_count
    slot_here = slot_here + row_id % rg_count
    order_now = jnp.zeros(shape, jnp.int32)
    source_now = jnp.zeros(shape, jnp.int32)
    for v in range(columns_all):
        slot = tile_table[v : v + 1, :]
        target = slot // columns_all // ap_count * rg_count + slot % columns_all // rg_count
        slot, target = jnp.broadcast_to(slot, shape), jnp.broadcast_to(target, shape)
        holder = line_id % ap_count * rg_count + v // rg_count
        source_now = source_now + jnp.where(slot == slot_here, holder, 0)
        mine = (target == row_id) & (holder == here_id)
        order_now = order_now + jnp.where(mine, line_id // ap_count * rg_count + v % rg_count, 0)
    diagonal = lax.broadcasted_iota(jnp.int32, (devices, LANES), 0) == lax.broadcasted_iota(
        jnp.int32, (devices, LANES), 1
    )
    for n, found in enumerate((order_now, source_now)):
        column = jnp.minimum(jnp.sum(found, axis=1, keepdims=True), devices - 1)
        column = jnp.where(diagonal, jnp.broadcast_to(column, (devices, LANES)), 0)
        routes_line[n : n + 1, :] = jnp.sum(column, axis=0, keepdims=True)
    routes_copy = pltpu.make_async_copy(routes_line, routes, routes_sem)
    routes_copy.start()
    routes_copy.wait()

    for side in range(2):

        @pl.when(has[side])
        def _():
            for copy in halo_copies(side):
                copy.wait_send()

    scale = root_half**levels

    def first_all(part):
        return pltpu.make_async_remote_copy(
            src_ref=first_out.at[part, pl.ds(0, ap_count - 1)],
            dst_ref=first_in.at[part, pl.ds(0, ap_count - 1)],
            send_sem=first_send.at[part],
            recv_sem=first_recv.at[part],
            device_id=(lax.rem(ap_here + 1, ap_count), rg_here),
            device_id_type=MESH,
        )

    def second_all(part):
        return pltpu.make_async_remote_copy(
            src_ref=second_out.at[part, pl.ds(0, devices - 1)],
            dst_ref=landed[part].at[pl.ds(0, devices - 1)],
            send_sem=second_send.at[part],
            recv_sem=second_recv.at[part],
            device_id=(lax.rem(ap_here + 1, ap_count), rg_here),
            device_id_type=MESH,
        )

    for part in range(2):
        first_in[part, ap_here] = first_out[part, ap_here]
        first_all(part).wait_recv()
        for k in range(blocks):
            column, at = k // per_chunk, k % per_chunk * LANES
            sums = hadamard([first_in[part, s, k].astype(jnp.float32) for s in range(ap_count)])
            for o, value in enumerate(sums):
                tiles[o * chunks + column, :, at : at + LANES] = (value * scale).astype(jnp.bfloat16)

        @pl.loop(0, devices)
        def _(d):
            second_out[part, d] = tiles[routes[0, d]]

        landed[part][here_id] = second_out[part, here_id]

        @pl.loop(1, devices)
        def _(step):
            peer = lax.rem(here_id + step, devices)
            pltpu.make_async_remote_copy(
                src_ref=second_out.at[part, peer],
                dst_ref=landed[part].at[here_id],
                send_sem=second_send.at[part],
                recv_sem=second_recv.at[part],
                device_id=(peer // rg_count, lax.rem(peer, rg_count)),
                device_id_type=MESH,
            ).start()

    for part in range(2):
        second_all(part).wait_recv()
        for i in range(ap_count):
            for j in range(chunks):
                placed[
                    part, i * tile_rows : (i + 1) * tile_rows, j * tile_bins : (j + 1) * tile_bins
                ] = landed[part][routes[1, i * chunks + j]].astype(jnp.float32)
    for part in range(2):
        first_all(part).wait_send()
        second_all(part).wait_send()


def per_device(raw_echoes, chirp, range_offsets, phases, tile_table):
    ap_count, rg_count = lax.axis_size("ap"), lax.axis_size("rg")
    devices = ap_count * rg_count
    levels = range_offsets.shape[0]
    _, pulses, range_bins = raw_echoes.shape
    distance = pulses * ap_count // 2**levels
    leaves = pulses // distance
    tile_rows = pulses // ap_count
    tile_bins = range_bins // rg_count

    placed = pl.pallas_call(
        functools.partial(image_kernel, levels, ap_count, rg_count),
        out_shape=pltpu.VMEM((2, pulses, range_bins), jnp.float32),
        in_specs=[pl.BlockSpec(memory_space=pltpu.HBM)] * 5,
        out_specs=pl.BlockSpec(memory_space=pltpu.VMEM),
        scratch_shapes=[
            pltpu.VMEM(chirp.shape, chirp.dtype),
            pltpu.VMEM(raw_echoes.shape, raw_echoes.dtype),
            pltpu.VMEM(range_offsets.shape, range_offsets.dtype),
            pltpu.VMEM(phases.shape, phases.dtype),
            pltpu.VMEM(tile_table.shape[::-1], tile_table.dtype),
            pltpu.VMEM((2, 2, pulses, LANES), jnp.bfloat16),
            pltpu.VMEM((2, levels, 2, LANES), jnp.int32),
            pltpu.VMEM((2, levels, 2, LANES), jnp.float32),
            pltpu.VMEM((2 * LANES, 4 * LANES), jnp.bfloat16),
            pltpu.VMEM((4 * levels, range_bins + LANES), jnp.float32),
            pltpu.VMEM((2, pulses, range_bins + LANES), jnp.float32),
            pltpu.VMEM((leaves, LANES), jnp.int32),
            pltpu.VMEM((leaves, LANES), jnp.float32),
            pltpu.VMEM((leaves, LANES), jnp.float32),
            pltpu.VMEM((2, pulses, LANES), jnp.float32),
            pltpu.VMEM((2, ap_count, range_bins // LANES, tile_rows, LANES), jnp.bfloat16),
            pltpu.VMEM((2, ap_count, range_bins // LANES, tile_rows, LANES), jnp.bfloat16),
            pltpu.VMEM((devices, tile_rows, tile_bins), jnp.bfloat16),
            pltpu.VMEM((2, devices, tile_rows, tile_bins), jnp.bfloat16),
            pltpu.VMEM((devices, tile_rows, tile_bins), jnp.bfloat16),
            pltpu.VMEM((devices, tile_rows, tile_bins), jnp.bfloat16),
            pltpu.VMEM((2, LANES), jnp.int32),
            pltpu.SMEM((2, LANES), jnp.int32),
            pltpu.SemaphoreType.DMA((2, 3)),
            pltpu.SemaphoreType.DMA((2, 3)),
            pltpu.SemaphoreType.DMA((2,)),
            pltpu.SemaphoreType.DMA((2,)),
            pltpu.SemaphoreType.DMA((2,)),
            pltpu.SemaphoreType.DMA((2,)),
            pltpu.SemaphoreType.DMA,
            pltpu.SemaphoreType.DMA((5,)),
        ],
        compiler_params=pltpu.CompilerParams(collective_id=0, has_side_effects=True, vmem_limit_bytes=24 * 2**20),
    )(
        *(
            pltpu.with_memory_space_constraint(operand, pltpu.HBM)
            for operand in (chirp, raw_echoes, range_offsets, phases, tile_table.T)
        )
    )
    return placed


def solution(mesh):
    placed = (P(None, "ap", "rg"), P(), P(None, None, "rg"), P(None, None, "rg"), P())
    return jax.shard_map(
        per_device, mesh=mesh, in_specs=placed, out_specs=P(None, "ap", "rg"), check_vma=False
    )
```

```python
import functools

import jax
import jax.numpy as jnp
from jax import lax
from jax.experimental import pallas as pl
from jax.experimental.pallas import tpu as pltpu
from jax.sharding import PartitionSpec as P

root_half = 0.7071067811865476
LANES = 128
MESH = pl.DeviceIdType.MESH


def hadamard(values):
    values = list(values)
    step = 1
    while step < len(values):
        for i in range(len(values)):
            if not i & step:
                a, b = values[i], values[i + step]
                values[i], values[i + step] = a + b, a - b
        step *= 2
    return values


def cos_sin(angle):
    turns = jnp.floor(angle * 0.6366197723675814 + 0.5)
    y = angle - turns * 1.5703125
    y = y - turns * 4.837512969970703e-4
    y = y - turns * 7.549789948768648e-8
    z = y * y
    sine = y * (1.0 + z * (-1 / 6 + z * (1 / 120 + z * (-1 / 5040 + z * (1 / 362880)))))
    cosine = 1.0 + z * (-0.5 + z * (1 / 24 + z * (-1 / 720 + z * (1 / 40320))))
    quarter = turns.astype(jnp.int32)
    odd = (quarter & 1) == 1
    c = jnp.where(odd, sine, cosine)
    s = jnp.where(odd, cosine, sine)
    c = jnp.where(((quarter + 1) & 2) == 2, -c, c)
    s = jnp.where((quarter & 2) == 2, -s, s)
    return c, s


def lane_pick(low, high, spot, in_low):
    return jnp.where(
        in_low,
        jnp.take_along_axis(low, spot, axis=1),
        jnp.take_along_axis(high, spot, axis=1),
    )


def filter_table(taps_ref):
    def spread(row):
        padded = jnp.concatenate([row, jnp.zeros_like(row)], axis=1)
        padded = jnp.broadcast_to(padded, (LANES, 2 * LANES))
        return pltpu.roll(padded, 0, 1, stride=1, stride_axis=0)

    real, imag = spread(taps_ref[0:1, :]), spread(taps_ref[1:2, :])
    return jnp.concatenate(
        [jnp.concatenate([real, imag], axis=1), jnp.concatenate([-imag, real], axis=1)], axis=0
    ).astype(jnp.bfloat16)


def image_kernel(
    levels,
    ap_count,
    rg_count,
    taps_hbm,
    raw_hbm,
    offsets_hbm,
    phases_hbm,
    tile_table_hbm,
    placed,
    taps,
    raw,
    offsets,
    phases,
    tile_table,
    raw_edges,
    offset_edges,
    phase_edges,
    weights,
    table,
    ext,
    spots,
    cosines,
    sines,
    terms,
    first_out,
    first_in,
    tiles,
    second_out,
    landed_real,
    landed_imag,
    routes_line,
    routes,
    halo_send,
    halo_recv,
    first_send,
    first_recv,
    second_send,
    second_recv,
    routes_sem,
    load_sem,
):
    ap_here, rg_here = lax.axis_index("ap"), lax.axis_index("rg")
    devices = ap_count * rg_count
    here_id = ap_here * rg_count + rg_here
    pulses, range_bins = raw.shape[1], raw.shape[2]
    tile_rows, tile_bins = tiles.shape[1], tiles.shape[2]
    chunks = range_bins // tile_bins
    distance = pulses * ap_count // 2**levels
    leaves = pulses // distance
    blocks = range_bins // LANES
    per_chunk = tile_bins // LANES
    first_bin = rg_here * range_bins
    total_bins = rg_count * range_bins
    rows_of = 2 * levels

    loads = [
        pltpu.make_async_copy(source, target, load_sem.at[n])
        for n, (source, target) in enumerate(
            (
                (taps_hbm, taps),
                (raw_hbm, raw),
                (offsets_hbm, offsets),
                (phases_hbm, phases),
                (tile_table_hbm, tile_table),
            )
        )
    ]
    barrier = pltpu.get_barrier_semaphore()
    for step in range(1, ap_count):
        at = lax.rem(ap_here + (step + ap_count // 2 - 1) % (ap_count - 1) + 1, ap_count)
        pl.semaphore_signal(barrier, inc=1, device_id=(at, rg_here), device_id_type=MESH)
    for step in range(1, rg_count):
        at = lax.rem(rg_here + step, rg_count)
        pl.semaphore_signal(barrier, inc=1, device_id=(ap_here, at), device_id_type=MESH)
    for load in loads:
        load.start()
    landed = (landed_real, landed_imag)

    loads[0].wait()
    weights[...] = filter_table(taps)
    for load in loads[1:]:
        load.wait()

    def columns_of(k):
        return pl.ds(pl.multiple_of(k * LANES, LANES), LANES)

    def raw_segment(part, k):
        if isinstance(k, int) and k == 0:
            return raw_edges[0, part]
        if isinstance(k, int) and k == blocks + 1:
            return raw_edges[1, part]
        return raw[part, :, columns_of(k - 1)]

    def filtered(k):
        window = jnp.concatenate(
            [raw_segment(0, k), raw_segment(0, k + 1), raw_segment(1, k), raw_segment(1, k + 1)], axis=1
        )
        both = lax.dot_general(
            window, weights[...], (((1,), (1,)), ((), ())), preferred_element_type=jnp.float32
        )
        ext[0, :, columns_of(k)] = both[:, :LANES]
        ext[1, :, columns_of(k)] = both[:, LANES:]

    def tabled(k):
        first_half = lax.broadcasted_iota(jnp.int32, (rows_of, LANES), 1) < LANES // 2
        for kind, (middle, edges) in enumerate(((offsets, offset_edges), (phases, phase_edges))):

            def segment(k):
                if isinstance(k, int) and k == 0:
                    piece = [edges[0, level] for level in range(levels)]
                elif isinstance(k, int) and k == blocks + 1:
                    piece = [edges[1, level] for level in range(levels)]
                else:
                    piece = [middle[level, :, columns_of(k - 1)] for level in range(levels)]
                piece = jnp.concatenate([part.astype(jnp.float32) for part in piece], axis=0)
                return pltpu.roll(piece, LANES // 2, 1)

            table[kind * rows_of : (kind + 1) * rows_of, columns_of(k)] = jnp.where(
                first_half, segment(k), segment(k + 1)
            )

    def halo_copies(side):
        columns = pl.ds(0, LANES) if side == 0 else pl.ds(range_bins - LANES, LANES)
        to = (ap_here, rg_here - 1 if side == 0 else rg_here + 1)
        pairs = (
            (raw.at[:, :, columns], raw_edges.at[1 - side]),
            (offsets.at[:, :, columns], offset_edges.at[1 - side]),
            (phases.at[:, :, columns], phase_edges.at[1 - side]),
        )
        return [
            pltpu.make_async_remote_copy(
                src_ref=source,
                dst_ref=target,
                send_sem=halo_send.at[side, n],
                recv_sem=halo_recv.at[1 - side, n],
                device_id=to,
                device_id_type=MESH,
            )
            for n, (source, target) in enumerate(pairs)
        ]

    has = (rg_here > 0, rg_here < rg_count - 1)

    leaf = lax.broadcasted_iota(jnp.int32, (leaves, LANES), 0) + ap_here * leaves
    lane = lax.broadcasted_iota(jnp.int32, (leaves, LANES), 1)
    radix = min(8, leaves)
    groups = leaves // radix

    def block(k):
        here = pl.multiple_of(k * LANES, LANES)
        after = pl.multiple_of(k * LANES + LANES, LANES)
        origin = first_bin + k * LANES - LANES // 2
        rel = lane + LANES // 2
        angle = jnp.zeros((leaves, LANES), jnp.float32)
        valid = jnp.ones((leaves, LANES), jnp.bool_)
        for level in reversed(range(levels)):
            upper = ((leaf >> level) & 1) == 1
            in_low = rel < LANES
            spot = rel & (LANES - 1)

            def looked_up(kind):
                row = kind * rows_of + level * 2
                pair = [
                    jnp.where(
                        upper,
                        table[row + 1 : row + 2, pl.ds(at, LANES)],
                        table[row : row + 1, pl.ds(at, LANES)],
                    )
                    for at in (here, after)
                ]
                return lane_pick(pair[0], pair[1], spot, in_low)

            offset = looked_up(0).astype(jnp.int32)
            angle = angle + looked_up(1)
            rel = rel + offset - 4
            where_now = rel + origin
            valid = valid & (where_now >= 0) & (where_now < total_bins)
        c, s = cos_sin(angle)
        spots[...] = rel
        cosines[...] = jnp.where(valid, c, 0.0)
        sines[...] = jnp.where(valid, s, 0.0)
        for group in range(groups):
            reals, imags = [], []
            for member in range(radix):
                one = group * radix + member
                rows = slice(one * distance, (one + 1) * distance)
                shape = (distance, LANES)
                at = jnp.broadcast_to(spots[one : one + 1, :], shape)
                cosine = jnp.broadcast_to(cosines[one : one + 1, :], shape)
                sine = jnp.broadcast_to(sines[one : one + 1, :], shape)
                in_low = at < LANES
                spot = at & (LANES - 1)
                real = lane_pick(
                    ext[0, rows, pl.ds(here, LANES)], ext[0, rows, pl.ds(after, LANES)], spot, in_low
                )
                imag = lane_pick(
                    ext[1, rows, pl.ds(here, LANES)], ext[1, rows, pl.ds(after, LANES)], spot, in_low
                )
                reals.append(real * cosine - imag * sine)
                imags.append(real * sine + imag * cosine)
            for part, values in enumerate((hadamard(reals), hadamard(imags))):
                for member, value in enumerate(values):
                    one = group * radix + member
                    terms[part, one * distance : (one + 1) * distance, :] = value
        span = radix * distance
        piece = min(tile_rows, span)
        for part in range(2):
            for begin in range(0, span, piece):
                sums = hadamard(
                    [terms[part, g * span + begin : g * span + begin + piece, :] for g in range(groups)]
                )
                for g, value in enumerate(sums):
                    row = g * span + begin
                    low = row % tile_rows
                    first_out[part, row // tile_rows, k, low : low + piece, :] = value.astype(
                        jnp.bfloat16
                    )

    def send_first(part, k):
        @pl.loop(1, ap_count)
        def _(step):
            peer = lax.rem(ap_here + step, ap_count)
            pltpu.make_async_remote_copy(
                src_ref=first_out.at[part, peer, k],
                dst_ref=first_in.at[part, ap_here, k],
                send_sem=first_send.at[part],
                recv_sem=first_recv.at[part],
                device_id=(peer, rg_here),
                device_id_type=MESH,
            ).start()

    def open_edges():
        pl.semaphore_wait(barrier, ap_count + rg_count - 2)
        for side in range(2):

            @pl.when(has[side])
            def _():
                for copy in halo_copies(side):
                    copy.start()

            @pl.when(jnp.logical_not(has[side]))
            def _():
                raw_edges[side] = jnp.zeros(raw_edges.shape[1:], raw_edges.dtype)
                offset_edges[side] = jnp.zeros(offset_edges.shape[1:], offset_edges.dtype)
                phase_edges[side] = jnp.zeros(phase_edges.shape[1:], phase_edges.dtype)

    if blocks > 2:
        filtered(1)
        tabled(1)

        @pl.loop(1, blocks - 1)
        def _(k):
            filtered(k + 1)
            tabled(k + 1)
            block(k)
            pl.when(k == 1)(open_edges)
            send_first(0, k)
            pl.when(k <= 2)(lambda: send_first(1, k))
    else:
        open_edges()
        for k in range(1, blocks):
            filtered(k)
            tabled(k)

    for side in range(2):

        @pl.when(has[side])
        def _():
            for copy in halo_copies(1 - side):
                copy.wait_recv()

    for k in (0, blocks):
        filtered(k)
        tabled(k)

    @pl.loop(0, min(blocks, 2))
    def _(i):
        block(i * (blocks - 1))
        send_first(0, i * (blocks - 1))

    send_first(1, 0)
    pl.loop(2 + 1, blocks)(lambda k: send_first(1, k))

    columns_all, lines = tile_table.shape
    shape = (devices, lines)
    row_id = lax.broadcasted_iota(jnp.int32, shape, 0)
    line_id = lax.broadcasted_iota(jnp.int32, shape, 1)
    slot_here = (ap_here * ap_count + row_id // rg_count) * columns_all + rg_here * rg_count
    slot_here = slot_here + row_id % rg_count
    order_now = jnp.zeros(shape, jnp.int32)
    source_now = jnp.zeros(shape, jnp.int32)
    for v in range(columns_all):
        slot = tile_table[v : v + 1, :]
        target = slot // columns_all // ap_count * rg_count + slot % columns_all // rg_count
        slot, target = jnp.broadcast_to(slot, shape), jnp.broadcast_to(target, shape)
        holder = line_id % ap_count * rg_count + v // rg_count
        source_now = source_now + jnp.where(slot == slot_here, holder, 0)
        mine = (target == row_id) & (holder == here_id)
        order_now = order_now + jnp.where(mine, line_id // ap_count * rg_count + v % rg_count, 0)
    diagonal = lax.broadcasted_iota(jnp.int32, (devices, LANES), 0) == lax.broadcasted_iota(
        jnp.int32, (devices, LANES), 1
    )
    for n, found in enumerate((order_now, source_now)):
        column = jnp.minimum(jnp.sum(found, axis=1, keepdims=True), devices - 1)
        column = jnp.where(diagonal, jnp.broadcast_to(column, (devices, LANES)), 0)
        routes_line[n : n + 1, :] = jnp.sum(column, axis=0, keepdims=True)
    routes_copy = pltpu.make_async_copy(routes_line, routes, routes_sem)
    routes_copy.start()
    routes_copy.wait()

    for side in range(2):

        @pl.when(has[side])
        def _():
            for copy in halo_copies(side):
                copy.wait_send()

    scale = root_half**levels

    def first_all(part):
        return pltpu.make_async_remote_copy(
            src_ref=first_out.at[part, pl.ds(0, ap_count - 1)],
            dst_ref=first_in.at[part, pl.ds(0, ap_count - 1)],
            send_sem=first_send.at[part],
            recv_sem=first_recv.at[part],
            device_id=(lax.rem(ap_here + 1, ap_count), rg_here),
            device_id_type=MESH,
        )

    def second_all(part):
        return pltpu.make_async_remote_copy(
            src_ref=second_out.at[part, pl.ds(0, devices - 1)],
            dst_ref=landed[part].at[pl.ds(0, devices - 1)],
            send_sem=second_send.at[part],
            recv_sem=second_recv.at[part],
            device_id=(lax.rem(ap_here + 1, ap_count), rg_here),
            device_id_type=MESH,
        )

    for part in range(2):
        first_in[part, ap_here] = first_out[part, ap_here]
        first_all(part).wait_recv()
        for k in range(blocks):
            column, at = k // per_chunk, k % per_chunk * LANES
            sums = hadamard([first_in[part, s, k].astype(jnp.float32) for s in range(ap_count)])
            for o, value in enumerate(sums):
                tiles[o * chunks + column, :, at : at + LANES] = (value * scale).astype(jnp.bfloat16)

        @pl.loop(0, devices)
        def _(d):
            second_out[part, d] = tiles[routes[0, d]]

        landed[part][here_id] = second_out[part, here_id]

        @pl.loop(1, devices)
        def _(step):
            peer = lax.rem(here_id + step, devices)
            pltpu.make_async_remote_copy(
                src_ref=second_out.at[part, peer],
                dst_ref=landed[part].at[here_id],
                send_sem=second_send.at[part],
                recv_sem=second_recv.at[part],
                device_id=(peer // rg_count, lax.rem(peer, rg_count)),
                device_id_type=MESH,
            ).start()

    for part in range(2):
        second_all(part).wait_recv()
        for i in range(ap_count):
            for j in range(chunks):
                placed[
                    part, i * tile_rows : (i + 1) * tile_rows, j * tile_bins : (j + 1) * tile_bins
                ] = landed[part][routes[1, i * chunks + j]].astype(jnp.float32)
    for part in range(2):
        first_all(part).wait_send()
        second_all(part).wait_send()


def per_device(raw_echoes, chirp, range_offsets, phases, tile_table):
    ap_count, rg_count = lax.axis_size("ap"), lax.axis_size("rg")
    devices = ap_count * rg_count
    levels = range_offsets.shape[0]
    _, pulses, range_bins = raw_echoes.shape
    distance = pulses * ap_count // 2**levels
    leaves = pulses // distance
    tile_rows = pulses // ap_count
    tile_bins = range_bins // rg_count

    placed = pl.pallas_call(
        functools.partial(image_kernel, levels, ap_count, rg_count),
        out_shape=pltpu.VMEM((2, pulses, range_bins), jnp.float32),
        in_specs=[pl.BlockSpec(memory_space=pltpu.HBM)] * 5,
        out_specs=pl.BlockSpec(memory_space=pltpu.VMEM),
        scratch_shapes=[
            pltpu.VMEM(chirp.shape, chirp.dtype),
            pltpu.VMEM(raw_echoes.shape, raw_echoes.dtype),
            pltpu.VMEM(range_offsets.shape, range_offsets.dtype),
            pltpu.VMEM(phases.shape, phases.dtype),
            pltpu.VMEM(tile_table.shape[::-1], tile_table.dtype),
            pltpu.VMEM((2, 2, pulses, LANES), jnp.bfloat16),
            pltpu.VMEM((2, levels, 2, LANES), jnp.int32),
            pltpu.VMEM((2, levels, 2, LANES), jnp.float32),
            pltpu.VMEM((2 * LANES, 4 * LANES), jnp.bfloat16),
            pltpu.VMEM((4 * levels, range_bins + LANES), jnp.float32),
            pltpu.VMEM((2, pulses, range_bins + LANES), jnp.float32),
            pltpu.VMEM((leaves, LANES), jnp.int32),
            pltpu.VMEM((leaves, LANES), jnp.float32),
            pltpu.VMEM((leaves, LANES), jnp.float32),
            pltpu.VMEM((2, pulses, LANES), jnp.float32),
            pltpu.VMEM((2, ap_count, range_bins // LANES, tile_rows, LANES), jnp.bfloat16),
            pltpu.VMEM((2, ap_count, range_bins // LANES, tile_rows, LANES), jnp.bfloat16),
            pltpu.VMEM((devices, tile_rows, tile_bins), jnp.bfloat16),
            pltpu.VMEM((2, devices, tile_rows, tile_bins), jnp.bfloat16),
            pltpu.VMEM((devices, tile_rows, tile_bins), jnp.bfloat16),
            pltpu.VMEM((devices, tile_rows, tile_bins), jnp.bfloat16),
            pltpu.VMEM((2, LANES), jnp.int32),
            pltpu.SMEM((2, LANES), jnp.int32),
            pltpu.SemaphoreType.DMA((2, 3)),
            pltpu.SemaphoreType.DMA((2, 3)),
            pltpu.SemaphoreType.DMA((2,)),
            pltpu.SemaphoreType.DMA((2,)),
            pltpu.SemaphoreType.DMA((2,)),
            pltpu.SemaphoreType.DMA((2,)),
            pltpu.SemaphoreType.DMA,
            pltpu.SemaphoreType.DMA((5,)),
        ],
        compiler_params=pltpu.CompilerParams(collective_id=0, has_side_effects=True, vmem_limit_bytes=24 * 2**20),
    )(
        *(
            pltpu.with_memory_space_constraint(operand, pltpu.HBM)
            for operand in (chirp, raw_echoes, range_offsets, phases, tile_table.T)
        )
    )
    return placed


def solution(mesh):
    placed = (P(None, "ap", "rg"), P(), P(None, None, "rg"), P(None, None, "rg"), P())
    return jax.shard_map(
        per_device, mesh=mesh, in_specs=placed, out_specs=P(None, "ap", "rg"), check_vma=False
    )
```

```python
import functools

import jax
import jax.numpy as jnp
from jax import lax
from jax.experimental import pallas as pl
from jax.experimental.pallas import tpu as pltpu
from jax.sharding import PartitionSpec as P

root_half = 0.7071067811865476
LANES = 128
MESH = pl.DeviceIdType.MESH


def hadamard(values):
    values = list(values)
    step = 1
    while step < len(values):
        for i in range(len(values)):
            if not i & step:
                a, b = values[i], values[i + step]
                values[i], values[i + step] = a + b, a - b
        step *= 2
    return values


def cos_sin(angle):
    turns = jnp.floor(angle * 0.6366197723675814 + 0.5)
    y = angle - turns * 1.5703125
    y = y - turns * 4.837512969970703e-4
    y = y - turns * 7.549789948768648e-8
    z = y * y
    sine = y * (1.0 + z * (-1 / 6 + z * (1 / 120 + z * (-1 / 5040 + z * (1 / 362880)))))
    cosine = 1.0 + z * (-0.5 + z * (1 / 24 + z * (-1 / 720 + z * (1 / 40320))))
    quarter = turns.astype(jnp.int32)
    odd = (quarter & 1) == 1
    c = jnp.where(odd, sine, cosine)
    s = jnp.where(odd, cosine, sine)
    c = jnp.where(((quarter + 1) & 2) == 2, -c, c)
    s = jnp.where((quarter & 2) == 2, -s, s)
    return c, s


def lane_pick(low, high, spot, in_low):
    return jnp.where(
        in_low,
        jnp.take_along_axis(low, spot, axis=1),
        jnp.take_along_axis(high, spot, axis=1),
    )


def filter_table(taps_ref):
    def spread(row):
        padded = jnp.concatenate([row, jnp.zeros_like(row)], axis=1)
        padded = jnp.broadcast_to(padded, (LANES, 2 * LANES))
        return pltpu.roll(padded, 0, 1, stride=1, stride_axis=0)

    real, imag = spread(taps_ref[0:1, :]), spread(taps_ref[1:2, :])
    return jnp.concatenate(
        [jnp.concatenate([real, imag], axis=1), jnp.concatenate([-imag, real], axis=1)], axis=0
    ).astype(jnp.bfloat16)


def image_kernel(
    levels,
    ap_count,
    rg_count,
    taps_hbm,
    raw_hbm,
    offsets_hbm,
    phases_hbm,
    tile_table_hbm,
    placed,
    taps,
    raw,
    offsets,
    phases,
    tile_table,
    raw_edges,
    offset_edges,
    phase_edges,
    weights,
    table,
    ext,
    spots,
    cosines,
    sines,
    terms,
    first_out,
    first_in,
    tiles,
    second_out,
    landed_real,
    landed_imag,
    routes_line,
    routes,
    halo_send,
    halo_recv,
    first_send,
    first_recv,
    second_send,
    second_recv,
    routes_sem,
    load_sem,
):
    ap_here, rg_here = lax.axis_index("ap"), lax.axis_index("rg")
    devices = ap_count * rg_count
    here_id = ap_here * rg_count + rg_here
    pulses, range_bins = raw.shape[1], raw.shape[2]
    tile_rows, tile_bins = tiles.shape[1], tiles.shape[2]
    chunks = range_bins // tile_bins
    distance = pulses * ap_count // 2**levels
    leaves = pulses // distance
    blocks = range_bins // LANES
    per_chunk = tile_bins // LANES
    first_bin = rg_here * range_bins
    total_bins = rg_count * range_bins
    rows_of = 2 * levels

    loads = [
        pltpu.make_async_copy(source, target, load_sem.at[n])
        for n, (source, target) in enumerate(
            (
                (taps_hbm, taps),
                (raw_hbm, raw),
                (offsets_hbm, offsets),
                (phases_hbm, phases),
                (tile_table_hbm, tile_table),
            )
        )
    ]
    barrier = pltpu.get_barrier_semaphore()
    for step in range(1, ap_count):
        at = lax.rem(ap_here + (step + ap_count // 2 - 1) % (ap_count - 1) + 1, ap_count)
        pl.semaphore_signal(barrier, inc=1, device_id=(at, rg_here), device_id_type=MESH)
    for step in range(1, rg_count):
        at = lax.rem(rg_here + step, rg_count)
        pl.semaphore_signal(barrier, inc=1, device_id=(ap_here, at), device_id_type=MESH)
    for load in loads:
        load.start()
    landed = (landed_real, landed_imag)

    loads[0].wait()
    weights[...] = filter_table(taps)
    for load in loads[1:]:
        load.wait()

    def columns_of(k):
        return pl.ds(pl.multiple_of(k * LANES, LANES), LANES)

    def raw_segment(part, k):
        if isinstance(k, int) and k == 0:
            return raw_edges[0, part]
        if isinstance(k, int) and k == blocks + 1:
            return raw_edges[1, part]
        return raw[part, :, columns_of(k - 1)]

    def filtered(k):
        window = jnp.concatenate(
            [raw_segment(0, k), raw_segment(0, k + 1), raw_segment(1, k), raw_segment(1, k + 1)], axis=1
        )
        both = lax.dot_general(
            window, weights[...], (((1,), (1,)), ((), ())), preferred_element_type=jnp.float32
        )
        ext[0, :, columns_of(k)] = both[:, :LANES]
        ext[1, :, columns_of(k)] = both[:, LANES:]

    def tabled(k):
        first_half = lax.broadcasted_iota(jnp.int32, (rows_of, LANES), 1) < LANES // 2
        for kind, (middle, edges) in enumerate(((offsets, offset_edges), (phases, phase_edges))):

            def segment(k):
                if isinstance(k, int) and k == 0:
                    piece = [edges[0, level] for level in range(levels)]
                elif isinstance(k, int) and k == blocks + 1:
                    piece = [edges[1, level] for level in range(levels)]
                else:
                    piece = [middle[level, :, columns_of(k - 1)] for level in range(levels)]
                piece = jnp.concatenate([part.astype(jnp.float32) for part in piece], axis=0)
                return pltpu.roll(piece, LANES // 2, 1)

            table[kind * rows_of : (kind + 1) * rows_of, columns_of(k)] = jnp.where(
                first_half, segment(k), segment(k + 1)
            )

    def halo_copies(side):
        columns = pl.ds(0, LANES) if side == 0 else pl.ds(range_bins - LANES, LANES)
        to = (ap_here, rg_here - 1 if side == 0 else rg_here + 1)
        pairs = (
            (raw.at[:, :, columns], raw_edges.at[1 - side]),
            (offsets.at[:, :, columns], offset_edges.at[1 - side]),
            (phases.at[:, :, columns], phase_edges.at[1 - side]),
        )
        return [
            pltpu.make_async_remote_copy(
                src_ref=source,
                dst_ref=target,
                send_sem=halo_send.at[side, n],
                recv_sem=halo_recv.at[1 - side, n],
                device_id=to,
                device_id_type=MESH,
            )
            for n, (source, target) in enumerate(pairs)
        ]

    has = (rg_here > 0, rg_here < rg_count - 1)

    leaf = lax.broadcasted_iota(jnp.int32, (leaves, LANES), 0) + ap_here * leaves
    lane = lax.broadcasted_iota(jnp.int32, (leaves, LANES), 1)
    radix = min(8, leaves)
    groups = leaves // radix

    def block(k):
        here = pl.multiple_of(k * LANES, LANES)
        after = pl.multiple_of(k * LANES + LANES, LANES)
        origin = first_bin + k * LANES - LANES // 2
        rel = lane + LANES // 2
        angle = jnp.zeros((leaves, LANES), jnp.float32)
        valid = jnp.ones((leaves, LANES), jnp.bool_)
        for level in reversed(range(levels)):
            upper = ((leaf >> level) & 1) == 1
            in_low = rel < LANES
            spot = rel & (LANES - 1)

            def looked_up(kind):
                row = kind * rows_of + level * 2
                pair = [
                    jnp.where(
                        upper,
                        table[row + 1 : row + 2, pl.ds(at, LANES)],
                        table[row : row + 1, pl.ds(at, LANES)],
                    )
                    for at in (here, after)
                ]
                return lane_pick(pair[0], pair[1], spot, in_low)

            offset = looked_up(0).astype(jnp.int32)
            angle = angle + looked_up(1)
            rel = rel + offset - 4
            where_now = rel + origin
            valid = valid & (where_now >= 0) & (where_now < total_bins)
        c, s = cos_sin(angle)
        spots[...] = rel
        cosines[...] = jnp.where(valid, c, 0.0)
        sines[...] = jnp.where(valid, s, 0.0)
        for group in range(groups):
            reals, imags = [], []
            for member in range(radix):
                one = group * radix + member
                rows = slice(one * distance, (one + 1) * distance)
                shape = (distance, LANES)
                at = jnp.broadcast_to(spots[one : one + 1, :], shape)
                cosine = jnp.broadcast_to(cosines[one : one + 1, :], shape)
                sine = jnp.broadcast_to(sines[one : one + 1, :], shape)
                in_low = at < LANES
                spot = at & (LANES - 1)
                real = lane_pick(
                    ext[0, rows, pl.ds(here, LANES)], ext[0, rows, pl.ds(after, LANES)], spot, in_low
                )
                imag = lane_pick(
                    ext[1, rows, pl.ds(here, LANES)], ext[1, rows, pl.ds(after, LANES)], spot, in_low
                )
                reals.append(real * cosine - imag * sine)
                imags.append(real * sine + imag * cosine)
            for part, values in enumerate((hadamard(reals), hadamard(imags))):
                for member, value in enumerate(values):
                    one = group * radix + member
                    terms[part, one * distance : (one + 1) * distance, :] = value
        span = radix * distance
        piece = min(tile_rows, span)
        for part in range(2):
            for begin in range(0, span, piece):
                sums = hadamard(
                    [terms[part, g * span + begin : g * span + begin + piece, :] for g in range(groups)]
                )
                for g, value in enumerate(sums):
                    row = g * span + begin
                    low = row % tile_rows
                    first_out[part, row // tile_rows, k, low : low + piece, :] = value.astype(
                        jnp.bfloat16
                    )

    def send_first(part, k):
        @pl.loop(1, ap_count)
        def _(step):
            peer = lax.rem(ap_here + step, ap_count)
            pltpu.make_async_remote_copy(
                src_ref=first_out.at[part, peer, k],
                dst_ref=first_in.at[part, ap_here, k],
                send_sem=first_send.at[part],
                recv_sem=first_recv.at[part],
                device_id=(peer, rg_here),
                device_id_type=MESH,
            ).start()

    def meet():
        pl.semaphore_wait(barrier, ap_count + rg_count - 2)

    def open_edges():
        for side in range(2):

            @pl.when(has[side])
            def _():
                for copy in halo_copies(side):
                    copy.start()

            @pl.when(jnp.logical_not(has[side]))
            def _():
                raw_edges[side] = jnp.zeros(raw_edges.shape[1:], raw_edges.dtype)
                offset_edges[side] = jnp.zeros(offset_edges.shape[1:], offset_edges.dtype)
                phase_edges[side] = jnp.zeros(phase_edges.shape[1:], phase_edges.dtype)

    if blocks > 2:
        filtered(1)
        tabled(1)

        @pl.loop(1, blocks - 1)
        def _(k):
            filtered(k + 1)
            tabled(k + 1)
            block(k)
            pl.when(k == 1)(meet)
            send_first(0, k)
            pl.when(k <= 2)(lambda: send_first(1, k))
            pl.when(k == 1)(open_edges)
    else:
        meet()
        open_edges()
        for k in range(1, blocks):
            filtered(k)
            tabled(k)

    for side in range(2):

        @pl.when(has[side])
        def _():
            for copy in halo_copies(1 - side):
                copy.wait_recv()

    for k in (0, blocks):
        filtered(k)
        tabled(k)

    @pl.loop(0, min(blocks, 2))
    def _(i):
        block(i * (blocks - 1))
        send_first(0, i * (blocks - 1))

    @pl.loop(1, ap_count)
    def _(step):
        peer = lax.rem(ap_here + step, ap_count)
        for first, last in ((0, 1), (3, blocks)):
            pltpu.make_async_remote_copy(
                src_ref=first_out.at[1, peer, pl.ds(first, last - first)],
                dst_ref=first_in.at[1, ap_here, pl.ds(first, last - first)],
                send_sem=first_send.at[1],
                recv_sem=first_recv.at[1],
                device_id=(peer, rg_here),
                device_id_type=MESH,
            ).start()


    columns_all, lines = tile_table.shape
    shape = (devices, lines)
    row_id = lax.broadcasted_iota(jnp.int32, shape, 0)
    line_id = lax.broadcasted_iota(jnp.int32, shape, 1)
    slot_here = (ap_here * ap_count + row_id // rg_count) * columns_all + rg_here * rg_count
    slot_here = slot_here + row_id % rg_count
    order_now = jnp.zeros(shape, jnp.int32)
    source_now = jnp.zeros(shape, jnp.int32)
    for v in range(columns_all):
        slot = tile_table[v : v + 1, :]
        target = slot // columns_all // ap_count * rg_count + slot % columns_all // rg_count
        slot, target = jnp.broadcast_to(slot, shape), jnp.broadcast_to(target, shape)
        holder = line_id % ap_count * rg_count + v // rg_count
        source_now = source_now + jnp.where(slot == slot_here, holder, 0)
        mine = (target == row_id) & (holder == here_id)
        order_now = order_now + jnp.where(mine, line_id // ap_count * rg_count + v % rg_count, 0)
    diagonal = lax.broadcasted_iota(jnp.int32, (devices, LANES), 0) == lax.broadcasted_iota(
        jnp.int32, (devices, LANES), 1
    )
    for n, found in enumerate((order_now, source_now)):
        column = jnp.minimum(jnp.sum(found, axis=1, keepdims=True), devices - 1)
        column = jnp.where(diagonal, jnp.broadcast_to(column, (devices, LANES)), 0)
        routes_line[n : n + 1, :] = jnp.sum(column, axis=0, keepdims=True)
    routes_copy = pltpu.make_async_copy(routes_line, routes, routes_sem)
    routes_copy.start()
    routes_copy.wait()

    for side in range(2):

        @pl.when(has[side])
        def _():
            for copy in halo_copies(side):
                copy.wait_send()

    scale = root_half**levels

    def first_all(part):
        return pltpu.make_async_remote_copy(
            src_ref=first_out.at[part, pl.ds(0, ap_count - 1)],
            dst_ref=first_in.at[part, pl.ds(0, ap_count - 1)],
            send_sem=first_send.at[part],
            recv_sem=first_recv.at[part],
            device_id=(lax.rem(ap_here + 1, ap_count), rg_here),
            device_id_type=MESH,
        )

    def second_all(part):
        return pltpu.make_async_remote_copy(
            src_ref=second_out.at[part, pl.ds(0, devices - 1)],
            dst_ref=landed[part].at[pl.ds(0, devices - 1)],
            send_sem=second_send.at[part],
            recv_sem=second_recv.at[part],
            device_id=(lax.rem(ap_here + 1, ap_count), rg_here),
            device_id_type=MESH,
        )

    for part in range(2):
        first_in[part, ap_here] = first_out[part, ap_here]
        first_all(part).wait_recv()
        for k in range(blocks):
            column, at = k // per_chunk, k % per_chunk * LANES
            sums = hadamard([first_in[part, s, k].astype(jnp.float32) for s in range(ap_count)])
            for o, value in enumerate(sums):
                tiles[o * chunks + column, :, at : at + LANES] = (value * scale).astype(jnp.bfloat16)

        @pl.loop(0, devices)
        def _(d):
            second_out[part, d] = tiles[routes[0, d]]

        landed[part][here_id] = second_out[part, here_id]

        @pl.loop(1, devices)
        def _(step):
            peer = lax.rem(here_id + step, devices)
            pltpu.make_async_remote_copy(
                src_ref=second_out.at[part, peer],
                dst_ref=landed[part].at[here_id],
                send_sem=second_send.at[part],
                recv_sem=second_recv.at[part],
                device_id=(peer // rg_count, lax.rem(peer, rg_count)),
                device_id_type=MESH,
            ).start()

    for part in range(2):
        second_all(part).wait_recv()
        for i in range(ap_count):
            for j in range(chunks):
                placed[
                    part, i * tile_rows : (i + 1) * tile_rows, j * tile_bins : (j + 1) * tile_bins
                ] = landed[part][routes[1, i * chunks + j]].astype(jnp.float32)
    for part in range(2):
        first_all(part).wait_send()
        second_all(part).wait_send()


def per_device(raw_echoes, chirp, range_offsets, phases, tile_table):
    ap_count, rg_count = lax.axis_size("ap"), lax.axis_size("rg")
    devices = ap_count * rg_count
    levels = range_offsets.shape[0]
    _, pulses, range_bins = raw_echoes.shape
    distance = pulses * ap_count // 2**levels
    leaves = pulses // distance
    tile_rows = pulses // ap_count
    tile_bins = range_bins // rg_count

    placed = pl.pallas_call(
        functools.partial(image_kernel, levels, ap_count, rg_count),
        out_shape=pltpu.VMEM((2, pulses, range_bins), jnp.float32),
        in_specs=[pl.BlockSpec(memory_space=pltpu.HBM)] * 5,
        out_specs=pl.BlockSpec(memory_space=pltpu.VMEM),
        scratch_shapes=[
            pltpu.VMEM(chirp.shape, chirp.dtype),
            pltpu.VMEM(raw_echoes.shape, raw_echoes.dtype),
            pltpu.VMEM(range_offsets.shape, range_offsets.dtype),
            pltpu.VMEM(phases.shape, phases.dtype),
            pltpu.VMEM(tile_table.shape[::-1], tile_table.dtype),
            pltpu.VMEM((2, 2, pulses, LANES), jnp.bfloat16),
            pltpu.VMEM((2, levels, 2, LANES), jnp.int32),
            pltpu.VMEM((2, levels, 2, LANES), jnp.float32),
            pltpu.VMEM((2 * LANES, 4 * LANES), jnp.bfloat16),
            pltpu.VMEM((4 * levels, range_bins + LANES), jnp.float32),
            pltpu.VMEM((2, pulses, range_bins + LANES), jnp.float32),
            pltpu.VMEM((leaves, LANES), jnp.int32),
            pltpu.VMEM((leaves, LANES), jnp.float32),
            pltpu.VMEM((leaves, LANES), jnp.float32),
            pltpu.VMEM((2, pulses, LANES), jnp.float32),
            pltpu.VMEM((2, ap_count, range_bins // LANES, tile_rows, LANES), jnp.bfloat16),
            pltpu.VMEM((2, ap_count, range_bins // LANES, tile_rows, LANES), jnp.bfloat16),
            pltpu.VMEM((devices, tile_rows, tile_bins), jnp.bfloat16),
            pltpu.VMEM((2, devices, tile_rows, tile_bins), jnp.bfloat16),
            pltpu.VMEM((devices, tile_rows, tile_bins), jnp.bfloat16),
            pltpu.VMEM((devices, tile_rows, tile_bins), jnp.bfloat16),
            pltpu.VMEM((2, LANES), jnp.int32),
            pltpu.SMEM((2, LANES), jnp.int32),
            pltpu.SemaphoreType.DMA((2, 3)),
            pltpu.SemaphoreType.DMA((2, 3)),
            pltpu.SemaphoreType.DMA((2,)),
            pltpu.SemaphoreType.DMA((2,)),
            pltpu.SemaphoreType.DMA((2,)),
            pltpu.SemaphoreType.DMA((2,)),
            pltpu.SemaphoreType.DMA,
            pltpu.SemaphoreType.DMA((5,)),
        ],
        compiler_params=pltpu.CompilerParams(collective_id=0, has_side_effects=True, vmem_limit_bytes=24 * 2**20),
    )(
        *(
            pltpu.with_memory_space_constraint(operand, pltpu.HBM)
            for operand in (chirp, raw_echoes, range_offsets, phases, tile_table.T)
        )
    )
    return placed


def solution(mesh):
    placed = (P(None, "ap", "rg"), P(), P(None, None, "rg"), P(None, None, "rg"), P())
    return jax.shard_map(
        per_device, mesh=mesh, in_specs=placed, out_specs=P(None, "ap", "rg"), check_vma=False
    )
```

```python
import functools

import jax
import jax.numpy as jnp
from jax import lax
from jax.experimental import pallas as pl
from jax.experimental.pallas import tpu as pltpu
from jax.sharding import PartitionSpec as P

root_half = 0.7071067811865476
LANES = 128
MESH = pl.DeviceIdType.MESH


def hadamard(values):
    values = list(values)
    step = 1
    while step < len(values):
        for i in range(len(values)):
            if not i & step:
                a, b = values[i], values[i + step]
                values[i], values[i + step] = a + b, a - b
        step *= 2
    return values


def cos_sin(angle):
    turns = jnp.floor(angle * 0.6366197723675814 + 0.5)
    y = angle - turns * 1.5703125
    y = y - turns * 4.837512969970703e-4
    y = y - turns * 7.549789948768648e-8
    z = y * y
    sine = y * (1.0 + z * (-1 / 6 + z * (1 / 120 + z * (-1 / 5040 + z * (1 / 362880)))))
    cosine = 1.0 + z * (-0.5 + z * (1 / 24 + z * (-1 / 720 + z * (1 / 40320))))
    quarter = turns.astype(jnp.int32)
    odd = (quarter & 1) == 1
    c = jnp.where(odd, sine, cosine)
    s = jnp.where(odd, cosine, sine)
    c = jnp.where(((quarter + 1) & 2) == 2, -c, c)
    s = jnp.where((quarter & 2) == 2, -s, s)
    return c, s


def lane_pick(low, high, spot, in_low):
    return jnp.where(
        in_low,
        jnp.take_along_axis(low, spot, axis=1),
        jnp.take_along_axis(high, spot, axis=1),
    )


def filter_table(taps_ref):
    def spread(row):
        padded = jnp.concatenate([row, jnp.zeros_like(row)], axis=1)
        padded = jnp.broadcast_to(padded, (LANES, 2 * LANES))
        return pltpu.roll(padded, 0, 1, stride=1, stride_axis=0)

    real, imag = spread(taps_ref[0:1, :]), spread(taps_ref[1:2, :])
    return jnp.concatenate(
        [jnp.concatenate([real, imag], axis=1), jnp.concatenate([-imag, real], axis=1)], axis=0
    ).astype(jnp.bfloat16)


def image_kernel(
    levels,
    ap_count,
    rg_count,
    taps_hbm,
    raw_hbm,
    offsets_hbm,
    phases_hbm,
    tile_table_hbm,
    placed,
    taps,
    raw,
    offsets,
    phases,
    tile_table,
    raw_edges,
    offset_edges,
    phase_edges,
    weights,
    table,
    ext,
    spots,
    cosines,
    sines,
    terms,
    first_out,
    first_in,
    tiles,
    second_out,
    landed_real,
    landed_imag,
    routes_line,
    routes,
    halo_send,
    halo_recv,
    first_send,
    first_recv,
    second_send,
    second_recv,
    routes_sem,
    load_sem,
    relayed,
):
    ap_here, rg_here = lax.axis_index("ap"), lax.axis_index("rg")
    devices = ap_count * rg_count
    here_id = ap_here * rg_count + rg_here
    pulses, range_bins = raw.shape[1], raw.shape[2]
    tile_rows, tile_bins = tiles.shape[1], tiles.shape[2]
    chunks = range_bins // tile_bins
    distance = pulses * ap_count // 2**levels
    leaves = pulses // distance
    blocks = range_bins // LANES
    per_chunk = tile_bins // LANES
    first_bin = rg_here * range_bins
    total_bins = rg_count * range_bins
    rows_of = 2 * levels

    loads = [
        pltpu.make_async_copy(source, target, load_sem.at[n])
        for n, (source, target) in enumerate(
            (
                (taps_hbm, taps),
                (raw_hbm, raw),
                (offsets_hbm, offsets),
                (phases_hbm, phases),
                (tile_table_hbm, tile_table),
            )
        )
    ]
    barrier = pltpu.get_barrier_semaphore()
    near = [1 << bit for bit in range((ap_count // 2 - 1).bit_length())]
    later = [mask for mask in range(1, ap_count // 2) if mask not in near]
    direct = [mask for mask in reversed(range(1, ap_count)) if mask not in later]
    rounds = len(near) - 1 if later else 0

    def greet(semaphore, mask):
        pl.semaphore_signal(semaphore, inc=1, device_id=(ap_here ^ mask, rg_here), device_id_type=MESH)

    for mask in direct:
        greet(barrier, mask)
    for step in range(1, rg_count):
        at = lax.rem(rg_here + step, rg_count)
        pl.semaphore_signal(barrier, inc=1, device_id=(ap_here, at), device_id_type=MESH)
    for load in loads:
        load.start()
    landed = (landed_real, landed_imag)

    loads[0].wait()
    weights[...] = filter_table(taps)
    for load in loads[1:]:
        load.wait()

    def columns_of(k):
        return pl.ds(pl.multiple_of(k * LANES, LANES), LANES)

    def raw_segment(part, k):
        if isinstance(k, int) and k == 0:
            return raw_edges[0, part]
        if isinstance(k, int) and k == blocks + 1:
            return raw_edges[1, part]
        return raw[part, :, columns_of(k - 1)]

    def filtered(k):
        window = jnp.concatenate(
            [raw_segment(0, k), raw_segment(0, k + 1), raw_segment(1, k), raw_segment(1, k + 1)], axis=1
        )
        both = lax.dot_general(
            window, weights[...], (((1,), (1,)), ((), ())), preferred_element_type=jnp.float32
        )
        ext[0, :, columns_of(k)] = both[:, :LANES]
        ext[1, :, columns_of(k)] = both[:, LANES:]

    def tabled(k):
        first_half = lax.broadcasted_iota(jnp.int32, (rows_of, LANES), 1) < LANES // 2
        for kind, (middle, edges) in enumerate(((offsets, offset_edges), (phases, phase_edges))):

            def segment(k):
                if isinstance(k, int) and k == 0:
                    piece = [edges[0, level] for level in range(levels)]
                elif isinstance(k, int) and k == blocks + 1:
                    piece = [edges[1, level] for level in range(levels)]
                else:
                    piece = [middle[level, :, columns_of(k - 1)] for level in range(levels)]
                piece = jnp.concatenate([part.astype(jnp.float32) for part in piece], axis=0)
                return pltpu.roll(piece, LANES // 2, 1)

            table[kind * rows_of : (kind + 1) * rows_of, columns_of(k)] = jnp.where(
                first_half, segment(k), segment(k + 1)
            )

    def halo_copies(side):
        columns = pl.ds(0, LANES) if side == 0 else pl.ds(range_bins - LANES, LANES)
        to = (ap_here, rg_here - 1 if side == 0 else rg_here + 1)
        pairs = (
            (raw.at[:, :, columns], raw_edges.at[1 - side]),
            (offsets.at[:, :, columns], offset_edges.at[1 - side]),
            (phases.at[:, :, columns], phase_edges.at[1 - side]),
        )
        return [
            pltpu.make_async_remote_copy(
                src_ref=source,
                dst_ref=target,
                send_sem=halo_send.at[side, n],
                recv_sem=halo_recv.at[1 - side, n],
                device_id=to,
                device_id_type=MESH,
            )
            for n, (source, target) in enumerate(pairs)
        ]

    has = (rg_here > 0, rg_here < rg_count - 1)

    leaf = lax.broadcasted_iota(jnp.int32, (leaves, LANES), 0) + ap_here * leaves
    lane = lax.broadcasted_iota(jnp.int32, (leaves, LANES), 1)
    radix = min(8, leaves)
    groups = leaves // radix

    def block(k):
        here = pl.multiple_of(k * LANES, LANES)
        after = pl.multiple_of(k * LANES + LANES, LANES)
        origin = first_bin + k * LANES - LANES // 2
        rel = lane + LANES // 2
        angle = jnp.zeros((leaves, LANES), jnp.float32)
        valid = jnp.ones((leaves, LANES), jnp.bool_)
        for level in reversed(range(levels)):
            upper = ((leaf >> level) & 1) == 1
            in_low = rel < LANES
            spot = rel & (LANES - 1)

            def looked_up(kind):
                row = kind * rows_of + level * 2
                pair = [
                    jnp.where(
                        upper,
                        table[row + 1 : row + 2, pl.ds(at, LANES)],
                        table[row : row + 1, pl.ds(at, LANES)],
                    )
                    for at in (here, after)
                ]
                return lane_pick(pair[0], pair[1], spot, in_low)

            offset = looked_up(0).astype(jnp.int32)
            angle = angle + looked_up(1)
            rel = rel + offset - 4
            where_now = rel + origin
            valid = valid & (where_now >= 0) & (where_now < total_bins)
        c, s = cos_sin(angle)
        spots[...] = rel
        cosines[...] = jnp.where(valid, c, 0.0)
        sines[...] = jnp.where(valid, s, 0.0)
        for group in range(groups):
            reals, imags = [], []
            for member in range(radix):
                one = group * radix + member
                rows = slice(one * distance, (one + 1) * distance)
                shape = (distance, LANES)
                at = jnp.broadcast_to(spots[one : one + 1, :], shape)
                cosine = jnp.broadcast_to(cosines[one : one + 1, :], shape)
                sine = jnp.broadcast_to(sines[one : one + 1, :], shape)
                in_low = at < LANES
                spot = at & (LANES - 1)
                real = lane_pick(
                    ext[0, rows, pl.ds(here, LANES)], ext[0, rows, pl.ds(after, LANES)], spot, in_low
                )
                imag = lane_pick(
                    ext[1, rows, pl.ds(here, LANES)], ext[1, rows, pl.ds(after, LANES)], spot, in_low
                )
                reals.append(real * cosine - imag * sine)
                imags.append(real * sine + imag * cosine)
            for part, values in enumerate((hadamard(reals), hadamard(imags))):
                for member, value in enumerate(values):
                    one = group * radix + member
                    terms[part, one * distance : (one + 1) * distance, :] = value
        span = radix * distance
        piece = min(tile_rows, span)
        for part in range(2):
            for begin in range(0, span, piece):
                sums = hadamard(
                    [terms[part, g * span + begin : g * span + begin + piece, :] for g in range(groups)]
                )
                for g, value in enumerate(sums):
                    row = g * span + begin
                    low = row % tile_rows
                    first_out[part, row // tile_rows, k, low : low + piece, :] = value.astype(
                        jnp.bfloat16
                    )

    def send_to(part, k, peer):
        pltpu.make_async_remote_copy(
            src_ref=first_out.at[part, peer, k],
            dst_ref=first_in.at[part, ap_here, k],
            send_sem=first_send.at[part],
            recv_sem=first_recv.at[part],
            device_id=(peer, rg_here),
            device_id_type=MESH,
        ).start()

    def send_first(part, k):
        @pl.loop(1, ap_count)
        def _(step):
            send_to(part, k, lax.rem(ap_here + step, ap_count))

    def send_direct(part, k):
        for mask in direct:
            send_to(part, k, ap_here ^ mask)

    def send_later(part, k):
        for mask in later:
            send_to(part, k, ap_here ^ mask)

    def tell(n):
        if n < rounds:
            for mask in near:
                greet(relayed.at[n], mask)

    def learn():
        for n in range(rounds):
            pl.semaphore_wait(relayed.at[n], len(near))
            tell(n + 1)

    def meet():
        pl.semaphore_wait(barrier, len(direct) + rg_count - 1)
        tell(0)

    def open_edges():
        for side in range(2):

            @pl.when(has[side])
            def _():
                for copy in halo_copies(side):
                    copy.start()

            @pl.when(jnp.logical_not(has[side]))
            def _():
                raw_edges[side] = jnp.zeros(raw_edges.shape[1:], raw_edges.dtype)
                offset_edges[side] = jnp.zeros(offset_edges.shape[1:], offset_edges.dtype)
                phase_edges[side] = jnp.zeros(phase_edges.shape[1:], phase_edges.dtype)

    if blocks > 2:
        filtered(1)
        tabled(1)

        @pl.loop(1, blocks - 1)
        def _(k):
            filtered(k + 1)
            tabled(k + 1)
            block(k)
            pl.when(k == 1)(meet)
            send_direct(0, k)
            pl.when(k <= 2)(lambda: send_direct(1, k))
            pl.when(k == 1)(open_edges)

        learn()
        if later:
            pl.loop(1, blocks - 1)(lambda k: send_later(0, k))
            pl.loop(1, 3)(lambda k: send_later(1, k))
    else:
        meet()
        learn()
        open_edges()
        for k in range(1, blocks):
            filtered(k)
            tabled(k)

    for side in range(2):

        @pl.when(has[side])
        def _():
            for copy in halo_copies(1 - side):
                copy.wait_recv()

    for k in (0, blocks):
        filtered(k)
        tabled(k)

    @pl.loop(0, min(blocks, 2))
    def _(i):
        block(i * (blocks - 1))
        send_first(0, i * (blocks - 1))

    @pl.loop(1, ap_count)
    def _(step):
        peer = lax.rem(ap_here + step, ap_count)
        for first, last in ((0, 1), (3, blocks)):
            pltpu.make_async_remote_copy(
                src_ref=first_out.at[1, peer, pl.ds(first, last - first)],
                dst_ref=first_in.at[1, ap_here, pl.ds(first, last - first)],
                send_sem=first_send.at[1],
                recv_sem=first_recv.at[1],
                device_id=(peer, rg_here),
                device_id_type=MESH,
            ).start()


    columns_all, lines = tile_table.shape
    shape = (devices, lines)
    row_id = lax.broadcasted_iota(jnp.int32, shape, 0)
    line_id = lax.broadcasted_iota(jnp.int32, shape, 1)
    slot_here = (ap_here * ap_count + row_id // rg_count) * columns_all + rg_here * rg_count
    slot_here = slot_here + row_id % rg_count
    order_now = jnp.zeros(shape, jnp.int32)
    source_now = jnp.zeros(shape, jnp.int32)
    for v in range(columns_all):
        slot = tile_table[v : v + 1, :]
        target = slot // columns_all // ap_count * rg_count + slot % columns_all // rg_count
        slot, target = jnp.broadcast_to(slot, shape), jnp.broadcast_to(target, shape)
        holder = line_id % ap_count * rg_count + v // rg_count
        source_now = source_now + jnp.where(slot == slot_here, holder, 0)
        mine = (target == row_id) & (holder == here_id)
        order_now = order_now + jnp.where(mine, line_id // ap_count * rg_count + v % rg_count, 0)
    diagonal = lax.broadcasted_iota(jnp.int32, (devices, LANES), 0) == lax.broadcasted_iota(
        jnp.int32, (devices, LANES), 1
    )
    for n, found in enumerate((order_now, source_now)):
        column = jnp.minimum(jnp.sum(found, axis=1, keepdims=True), devices - 1)
        column = jnp.where(diagonal, jnp.broadcast_to(column, (devices, LANES)), 0)
        routes_line[n : n + 1, :] = jnp.sum(column, axis=0, keepdims=True)
    routes_copy = pltpu.make_async_copy(routes_line, routes, routes_sem)
    routes_copy.start()
    routes_copy.wait()

    for side in range(2):

        @pl.when(has[side])
        def _():
            for copy in halo_copies(side):
                copy.wait_send()

    scale = root_half**levels

    def first_all(part):
        return pltpu.make_async_remote_copy(
            src_ref=first_out.at[part, pl.ds(0, ap_count - 1)],
            dst_ref=first_in.at[part, pl.ds(0, ap_count - 1)],
            send_sem=first_send.at[part],
            recv_sem=first_recv.at[part],
            device_id=(lax.rem(ap_here + 1, ap_count), rg_here),
            device_id_type=MESH,
        )

    def second_all(part):
        return pltpu.make_async_remote_copy(
            src_ref=second_out.at[part, pl.ds(0, devices - 1)],
            dst_ref=landed[part].at[pl.ds(0, devices - 1)],
            send_sem=second_send.at[part],
            recv_sem=second_recv.at[part],
            device_id=(lax.rem(ap_here + 1, ap_count), rg_here),
            device_id_type=MESH,
        )

    for part in range(2):
        first_in[part, ap_here] = first_out[part, ap_here]
        first_all(part).wait_recv()
        for k in range(blocks):
            column, at = k // per_chunk, k % per_chunk * LANES
            sums = hadamard([first_in[part, s, k].astype(jnp.float32) for s in range(ap_count)])
            for o, value in enumerate(sums):
                tiles[o * chunks + column, :, at : at + LANES] = (value * scale).astype(jnp.bfloat16)

        @pl.loop(0, devices)
        def _(d):
            second_out[part, d] = tiles[routes[0, d]]

        landed[part][here_id] = second_out[part, here_id]

        @pl.loop(1, devices)
        def _(step):
            peer = lax.rem(here_id + step, devices)
            pltpu.make_async_remote_copy(
                src_ref=second_out.at[part, peer],
                dst_ref=landed[part].at[here_id],
                send_sem=second_send.at[part],
                recv_sem=second_recv.at[part],
                device_id=(peer // rg_count, lax.rem(peer, rg_count)),
                device_id_type=MESH,
            ).start()

    for part in range(2):
        second_all(part).wait_recv()
        for i in range(ap_count):
            for j in range(chunks):
                placed[
                    part, i * tile_rows : (i + 1) * tile_rows, j * tile_bins : (j + 1) * tile_bins
                ] = landed[part][routes[1, i * chunks + j]].astype(jnp.float32)
    for part in range(2):
        first_all(part).wait_send()
        second_all(part).wait_send()


def per_device(raw_echoes, chirp, range_offsets, phases, tile_table):
    ap_count, rg_count = lax.axis_size("ap"), lax.axis_size("rg")
    devices = ap_count * rg_count
    levels = range_offsets.shape[0]
    _, pulses, range_bins = raw_echoes.shape
    distance = pulses * ap_count // 2**levels
    leaves = pulses // distance
    tile_rows = pulses // ap_count
    tile_bins = range_bins // rg_count

    placed = pl.pallas_call(
        functools.partial(image_kernel, levels, ap_count, rg_count),
        out_shape=pltpu.VMEM((2, pulses, range_bins), jnp.float32),
        in_specs=[pl.BlockSpec(memory_space=pltpu.HBM)] * 5,
        out_specs=pl.BlockSpec(memory_space=pltpu.VMEM),
        scratch_shapes=[
            pltpu.VMEM(chirp.shape, chirp.dtype),
            pltpu.VMEM(raw_echoes.shape, raw_echoes.dtype),
            pltpu.VMEM(range_offsets.shape, range_offsets.dtype),
            pltpu.VMEM(phases.shape, phases.dtype),
            pltpu.VMEM(tile_table.shape[::-1], tile_table.dtype),
            pltpu.VMEM((2, 2, pulses, LANES), jnp.bfloat16),
            pltpu.VMEM((2, levels, 2, LANES), jnp.int32),
            pltpu.VMEM((2, levels, 2, LANES), jnp.float32),
            pltpu.VMEM((2 * LANES, 4 * LANES), jnp.bfloat16),
            pltpu.VMEM((4 * levels, range_bins + LANES), jnp.float32),
            pltpu.VMEM((2, pulses, range_bins + LANES), jnp.float32),
            pltpu.VMEM((leaves, LANES), jnp.int32),
            pltpu.VMEM((leaves, LANES), jnp.float32),
            pltpu.VMEM((leaves, LANES), jnp.float32),
            pltpu.VMEM((2, pulses, LANES), jnp.float32),
            pltpu.VMEM((2, ap_count, range_bins // LANES, tile_rows, LANES), jnp.bfloat16),
            pltpu.VMEM((2, ap_count, range_bins // LANES, tile_rows, LANES), jnp.bfloat16),
            pltpu.VMEM((devices, tile_rows, tile_bins), jnp.bfloat16),
            pltpu.VMEM((2, devices, tile_rows, tile_bins), jnp.bfloat16),
            pltpu.VMEM((devices, tile_rows, tile_bins), jnp.bfloat16),
            pltpu.VMEM((devices, tile_rows, tile_bins), jnp.bfloat16),
            pltpu.VMEM((2, LANES), jnp.int32),
            pltpu.SMEM((2, LANES), jnp.int32),
            pltpu.SemaphoreType.DMA((2, 3)),
            pltpu.SemaphoreType.DMA((2, 3)),
            pltpu.SemaphoreType.DMA((2,)),
            pltpu.SemaphoreType.DMA((2,)),
            pltpu.SemaphoreType.DMA((2,)),
            pltpu.SemaphoreType.DMA((2,)),
            pltpu.SemaphoreType.DMA,
            pltpu.SemaphoreType.DMA((5,)),
            pltpu.SemaphoreType.REGULAR((max(ap_count.bit_length() - 3, 1),)),
        ],
        compiler_params=pltpu.CompilerParams(collective_id=0, has_side_effects=True, vmem_limit_bytes=24 * 2**20),
    )(
        *(
            pltpu.with_memory_space_constraint(operand, pltpu.HBM)
            for operand in (chirp, raw_echoes, range_offsets, phases, tile_table.T)
        )
    )
    return placed


def solution(mesh):
    placed = (P(None, "ap", "rg"), P(), P(None, None, "rg"), P(None, None, "rg"), P())
    return jax.shard_map(
        per_device, mesh=mesh, in_specs=placed, out_specs=P(None, "ap", "rg"), check_vma=False
    )
```

```python
import functools

import jax
import jax.numpy as jnp
from jax import lax
from jax.experimental import pallas as pl
from jax.experimental.pallas import tpu as pltpu
from jax.sharding import PartitionSpec as P

root_half = 0.7071067811865476
LANES = 128
MESH = pl.DeviceIdType.MESH


def hadamard(values):
    values = list(values)
    step = 1
    while step < len(values):
        for i in range(len(values)):
            if not i & step:
                a, b = values[i], values[i + step]
                values[i], values[i + step] = a + b, a - b
        step *= 2
    return values


def cos_sin(angle):
    turns = jnp.floor(angle * 0.6366197723675814 + 0.5)
    y = angle - turns * 1.5703125
    y = y - turns * 4.837512969970703e-4
    y = y - turns * 7.549789948768648e-8
    z = y * y
    sine = y * (1.0 + z * (-1 / 6 + z * (1 / 120 + z * (-1 / 5040 + z * (1 / 362880)))))
    cosine = 1.0 + z * (-0.5 + z * (1 / 24 + z * (-1 / 720 + z * (1 / 40320))))
    quarter = turns.astype(jnp.int32)
    odd = (quarter & 1) == 1
    c = jnp.where(odd, sine, cosine)
    s = jnp.where(odd, cosine, sine)
    c = jnp.where(((quarter + 1) & 2) == 2, -c, c)
    s = jnp.where((quarter & 2) == 2, -s, s)
    return c, s


def lane_pick(low, high, spot, in_low):
    return jnp.where(
        in_low,
        jnp.take_along_axis(low, spot, axis=1),
        jnp.take_along_axis(high, spot, axis=1),
    )


def filter_table(taps_ref):
    def spread(row):
        padded = jnp.concatenate([row, jnp.zeros_like(row)], axis=1)
        padded = jnp.broadcast_to(padded, (LANES, 2 * LANES))
        return pltpu.roll(padded, 0, 1, stride=1, stride_axis=0)

    real, imag = spread(taps_ref[0:1, :]), spread(taps_ref[1:2, :])
    return jnp.concatenate(
        [jnp.concatenate([real, imag], axis=1), jnp.concatenate([-imag, real], axis=1)], axis=0
    ).astype(jnp.bfloat16)


def image_kernel(
    levels,
    ap_count,
    rg_count,
    taps_hbm,
    raw_hbm,
    offsets_hbm,
    phases_hbm,
    tile_table_hbm,
    placed,
    taps,
    raw,
    offsets,
    phases,
    tile_table,
    raw_edges,
    offset_edges,
    phase_edges,
    weights,
    table,
    ext,
    spots,
    cosines,
    sines,
    terms,
    first_out,
    first_in,
    tiles,
    second_out,
    landed_real,
    landed_imag,
    routes_line,
    routes,
    halo_send,
    halo_recv,
    first_send,
    first_recv,
    second_send,
    second_recv,
    routes_sem,
    load_sem,
):
    ap_here, rg_here = lax.axis_index("ap"), lax.axis_index("rg")
    devices = ap_count * rg_count
    here_id = ap_here * rg_count + rg_here
    pulses, range_bins = raw.shape[1], raw.shape[2]
    tile_rows, tile_bins = tiles.shape[1], tiles.shape[2]
    chunks = range_bins // tile_bins
    distance = pulses * ap_count // 2**levels
    leaves = pulses // distance
    blocks = range_bins // LANES
    per_chunk = tile_bins // LANES
    first_bin = rg_here * range_bins
    total_bins = rg_count * range_bins
    rows_of = 2 * levels

    loads = [
        pltpu.make_async_copy(source, target, load_sem.at[n])
        for n, (source, target) in enumerate(
            (
                (taps_hbm, taps),
                (raw_hbm, raw),
                (offsets_hbm, offsets),
                (phases_hbm, phases),
                (tile_table_hbm, tile_table),
            )
        )
    ]
    barrier = pltpu.get_barrier_semaphore()
    for step in range(1, ap_count):
        at = lax.rem(ap_here + (step + ap_count // 2 - 1) % (ap_count - 1) + 1, ap_count)
        pl.semaphore_signal(barrier, inc=1, device_id=(at, rg_here), device_id_type=MESH)
    for step in range(1, rg_count):
        at = lax.rem(rg_here + step, rg_count)
        pl.semaphore_signal(barrier, inc=1, device_id=(ap_here, at), device_id_type=MESH)
    for load in loads:
        load.start()
    landed = (landed_real, landed_imag)

    loads[0].wait()
    weights[...] = filter_table(taps)
    for load in loads[1:]:
        load.wait()

    def columns_of(k):
        return pl.ds(pl.multiple_of(k * LANES, LANES), LANES)

    def raw_segment(part, k):
        if isinstance(k, int) and k == 0:
            return raw_edges[0, part]
        if isinstance(k, int) and k == blocks + 1:
            return raw_edges[1, part]
        return raw[part, :, columns_of(k - 1)]

    def filtered(k):
        window = jnp.concatenate(
            [raw_segment(0, k), raw_segment(0, k + 1), raw_segment(1, k), raw_segment(1, k + 1)], axis=1
        )
        both = lax.dot_general(
            window, weights[...], (((1,), (1,)), ((), ())), preferred_element_type=jnp.float32
        )
        ext[0, :, columns_of(k)] = both[:, :LANES]
        ext[1, :, columns_of(k)] = both[:, LANES:]

    def tabled(k):
        first_half = lax.broadcasted_iota(jnp.int32, (rows_of, LANES), 1) < LANES // 2
        for kind, (middle, edges) in enumerate(((offsets, offset_edges), (phases, phase_edges))):

            def segment(k):
                if isinstance(k, int) and k == 0:
                    piece = [edges[0, level] for level in range(levels)]
                elif isinstance(k, int) and k == blocks + 1:
                    piece = [edges[1, level] for level in range(levels)]
                else:
                    piece = [middle[level, :, columns_of(k - 1)] for level in range(levels)]
                piece = jnp.concatenate([part.astype(jnp.float32) for part in piece], axis=0)
                return pltpu.roll(piece, LANES // 2, 1)

            table[kind * rows_of : (kind + 1) * rows_of, columns_of(k)] = jnp.where(
                first_half, segment(k), segment(k + 1)
            )

    def halo_copies(side):
        columns = pl.ds(0, LANES) if side == 0 else pl.ds(range_bins - LANES, LANES)
        to = (ap_here, rg_here - 1 if side == 0 else rg_here + 1)
        pairs = (
            (raw.at[:, :, columns], raw_edges.at[1 - side]),
            (offsets.at[:, :, columns], offset_edges.at[1 - side]),
            (phases.at[:, :, columns], phase_edges.at[1 - side]),
        )
        return [
            pltpu.make_async_remote_copy(
                src_ref=source,
                dst_ref=target,
                send_sem=halo_send.at[side, n],
                recv_sem=halo_recv.at[1 - side, n],
                device_id=to,
                device_id_type=MESH,
            )
            for n, (source, target) in enumerate(pairs)
        ]

    has = (rg_here > 0, rg_here < rg_count - 1)

    leaf = lax.broadcasted_iota(jnp.int32, (leaves, LANES), 0) + ap_here * leaves
    lane = lax.broadcasted_iota(jnp.int32, (leaves, LANES), 1)
    radix = min(8, leaves)
    groups = leaves // radix

    def block(k):
        here = pl.multiple_of(k * LANES, LANES)
        after = pl.multiple_of(k * LANES + LANES, LANES)
        origin = first_bin + k * LANES - LANES // 2
        rel = lane + LANES // 2
        angle = jnp.zeros((leaves, LANES), jnp.float32)
        valid = jnp.ones((leaves, LANES), jnp.bool_)
        for level in reversed(range(levels)):
            upper = ((leaf >> level) & 1) == 1
            in_low = rel < LANES
            spot = rel & (LANES - 1)

            def looked_up(kind):
                row = kind * rows_of + level * 2
                pair = [
                    jnp.where(
                        upper,
                        table[row + 1 : row + 2, pl.ds(at, LANES)],
                        table[row : row + 1, pl.ds(at, LANES)],
                    )
                    for at in (here, after)
                ]
                return lane_pick(pair[0], pair[1], spot, in_low)

            offset = looked_up(0).astype(jnp.int32)
            angle = angle + looked_up(1)
            rel = rel + offset - 4
            where_now = rel + origin
            valid = valid & (where_now >= 0) & (where_now < total_bins)
        c, s = cos_sin(angle)
        spots[...] = rel
        cosines[...] = jnp.where(valid, c, 0.0)
        sines[...] = jnp.where(valid, s, 0.0)
        for group in range(groups):
            reals, imags = [], []
            for member in range(radix):
                one = group * radix + member
                rows = slice(one * distance, (one + 1) * distance)
                shape = (distance, LANES)
                at = jnp.broadcast_to(spots[one : one + 1, :], shape)
                cosine = jnp.broadcast_to(cosines[one : one + 1, :], shape)
                sine = jnp.broadcast_to(sines[one : one + 1, :], shape)
                in_low = at < LANES
                spot = at & (LANES - 1)
                real = lane_pick(
                    ext[0, rows, pl.ds(here, LANES)], ext[0, rows, pl.ds(after, LANES)], spot, in_low
                )
                imag = lane_pick(
                    ext[1, rows, pl.ds(here, LANES)], ext[1, rows, pl.ds(after, LANES)], spot, in_low
                )
                reals.append(real * cosine - imag * sine)
                imags.append(real * sine + imag * cosine)
            for part, values in enumerate((hadamard(reals), hadamard(imags))):
                for member, value in enumerate(values):
                    one = group * radix + member
                    terms[part, one * distance : (one + 1) * distance, :] = value
        span = radix * distance
        piece = min(tile_rows, span)
        for part in range(2):
            for begin in range(0, span, piece):
                sums = hadamard(
                    [terms[part, g * span + begin : g * span + begin + piece, :] for g in range(groups)]
                )
                for g, value in enumerate(sums):
                    row = g * span + begin
                    low = row % tile_rows
                    first_out[part, row // tile_rows, k, low : low + piece, :] = value.astype(
                        jnp.bfloat16
                    )

    def send_first(part, k):
        @pl.loop(1, ap_count)
        def _(step):
            peer = lax.rem(ap_here + step, ap_count)
            pltpu.make_async_remote_copy(
                src_ref=first_out.at[part, peer, k],
                dst_ref=first_in.at[part, ap_here, k],
                send_sem=first_send.at[part],
                recv_sem=first_recv.at[part],
                device_id=(peer, rg_here),
                device_id_type=MESH,
            ).start()

    def meet():
        pl.semaphore_wait(barrier, ap_count + rg_count - 2)

    def open_edges():
        for side in range(2):

            @pl.when(has[side])
            def _():
                for copy in halo_copies(side):
                    copy.start()

            @pl.when(jnp.logical_not(has[side]))
            def _():
                raw_edges[side] = jnp.zeros(raw_edges.shape[1:], raw_edges.dtype)
                offset_edges[side] = jnp.zeros(offset_edges.shape[1:], offset_edges.dtype)
                phase_edges[side] = jnp.zeros(phase_edges.shape[1:], phase_edges.dtype)

    def prepare(k):
        filtered(k)
        tabled(k)

    if blocks > 2:
        prepare(1)
        prepare(2)

        @pl.loop(1, blocks - 1)
        def _(k):
            block(k)
            pl.when(k < blocks - 2)(lambda: prepare(k + 2))
            pl.when(k == 1)(meet)
            send_first(0, k)
            pl.when(k <= 2)(lambda: send_first(1, k))
            pl.when(k == 1)(open_edges)
    else:
        meet()
        open_edges()
        for k in range(1, blocks):
            filtered(k)
            tabled(k)

    for side in range(2):

        @pl.when(has[side])
        def _():
            for copy in halo_copies(1 - side):
                copy.wait_recv()

    for k in (0, blocks):
        filtered(k)
        tabled(k)

    @pl.loop(0, min(blocks, 2))
    def _(i):
        block(i * (blocks - 1))
        send_first(0, i * (blocks - 1))

    send_first(1, 0)
    pl.loop(2 + 1, blocks)(lambda k: send_first(1, k))

    columns_all, lines = tile_table.shape
    shape = (devices, lines)
    row_id = lax.broadcasted_iota(jnp.int32, shape, 0)
    line_id = lax.broadcasted_iota(jnp.int32, shape, 1)
    slot_here = (ap_here * ap_count + row_id // rg_count) * columns_all + rg_here * rg_count
    slot_here = slot_here + row_id % rg_count
    order_now = jnp.zeros(shape, jnp.int32)
    source_now = jnp.zeros(shape, jnp.int32)
    for v in range(columns_all):
        slot = tile_table[v : v + 1, :]
        target = slot // columns_all // ap_count * rg_count + slot % columns_all // rg_count
        slot, target = jnp.broadcast_to(slot, shape), jnp.broadcast_to(target, shape)
        holder = line_id % ap_count * rg_count + v // rg_count
        source_now = source_now + jnp.where(slot == slot_here, holder, 0)
        mine = (target == row_id) & (holder == here_id)
        order_now = order_now + jnp.where(mine, line_id // ap_count * rg_count + v % rg_count, 0)
    diagonal = lax.broadcasted_iota(jnp.int32, (devices, LANES), 0) == lax.broadcasted_iota(
        jnp.int32, (devices, LANES), 1
    )
    for n, found in enumerate((order_now, source_now)):
        column = jnp.minimum(jnp.sum(found, axis=1, keepdims=True), devices - 1)
        column = jnp.where(diagonal, jnp.broadcast_to(column, (devices, LANES)), 0)
        routes_line[n : n + 1, :] = jnp.sum(column, axis=0, keepdims=True)
    routes_copy = pltpu.make_async_copy(routes_line, routes, routes_sem)
    routes_copy.start()
    routes_copy.wait()

    for side in range(2):

        @pl.when(has[side])
        def _():
            for copy in halo_copies(side):
                copy.wait_send()

    scale = root_half**levels

    def first_all(part):
        return pltpu.make_async_remote_copy(
            src_ref=first_out.at[part, pl.ds(0, ap_count - 1)],
            dst_ref=first_in.at[part, pl.ds(0, ap_count - 1)],
            send_sem=first_send.at[part],
            recv_sem=first_recv.at[part],
            device_id=(lax.rem(ap_here + 1, ap_count), rg_here),
            device_id_type=MESH,
        )

    def second_all(part):
        return pltpu.make_async_remote_copy(
            src_ref=second_out.at[part, pl.ds(0, devices - 1)],
            dst_ref=landed[part].at[pl.ds(0, devices - 1)],
            send_sem=second_send.at[part],
            recv_sem=second_recv.at[part],
            device_id=(lax.rem(ap_here + 1, ap_count), rg_here),
            device_id_type=MESH,
        )

    for part in range(2):
        first_in[part, ap_here] = first_out[part, ap_here]
        first_all(part).wait_recv()
        for k in range(blocks):
            column, at = k // per_chunk, k % per_chunk * LANES
            sums = hadamard([first_in[part, s, k].astype(jnp.float32) for s in range(ap_count)])
            for o, value in enumerate(sums):
                tiles[o * chunks + column, :, at : at + LANES] = (value * scale).astype(jnp.bfloat16)

        @pl.loop(0, devices)
        def _(d):
            second_out[part, d] = tiles[routes[0, d]]

        landed[part][here_id] = second_out[part, here_id]

        @pl.loop(1, devices)
        def _(step):
            peer = lax.rem(here_id + step, devices)
            pltpu.make_async_remote_copy(
                src_ref=second_out.at[part, peer],
                dst_ref=landed[part].at[here_id],
                send_sem=second_send.at[part],
                recv_sem=second_recv.at[part],
                device_id=(peer // rg_count, lax.rem(peer, rg_count)),
                device_id_type=MESH,
            ).start()

    for part in range(2):
        second_all(part).wait_recv()
        for i in range(ap_count):
            for j in range(chunks):
                placed[
                    part, i * tile_rows : (i + 1) * tile_rows, j * tile_bins : (j + 1) * tile_bins
                ] = landed[part][routes[1, i * chunks + j]].astype(jnp.float32)
    for part in range(2):
        first_all(part).wait_send()
        second_all(part).wait_send()


def per_device(raw_echoes, chirp, range_offsets, phases, tile_table):
    ap_count, rg_count = lax.axis_size("ap"), lax.axis_size("rg")
    devices = ap_count * rg_count
    levels = range_offsets.shape[0]
    _, pulses, range_bins = raw_echoes.shape
    distance = pulses * ap_count // 2**levels
    leaves = pulses // distance
    tile_rows = pulses // ap_count
    tile_bins = range_bins // rg_count

    placed = pl.pallas_call(
        functools.partial(image_kernel, levels, ap_count, rg_count),
        out_shape=pltpu.VMEM((2, pulses, range_bins), jnp.float32),
        in_specs=[pl.BlockSpec(memory_space=pltpu.HBM)] * 5,
        out_specs=pl.BlockSpec(memory_space=pltpu.VMEM),
        scratch_shapes=[
            pltpu.VMEM(chirp.shape, chirp.dtype),
            pltpu.VMEM(raw_echoes.shape, raw_echoes.dtype),
            pltpu.VMEM(range_offsets.shape, range_offsets.dtype),
            pltpu.VMEM(phases.shape, phases.dtype),
            pltpu.VMEM(tile_table.shape[::-1], tile_table.dtype),
            pltpu.VMEM((2, 2, pulses, LANES), jnp.bfloat16),
            pltpu.VMEM((2, levels, 2, LANES), jnp.int32),
            pltpu.VMEM((2, levels, 2, LANES), jnp.float32),
            pltpu.VMEM((2 * LANES, 4 * LANES), jnp.bfloat16),
            pltpu.VMEM((4 * levels, range_bins + LANES), jnp.float32),
            pltpu.VMEM((2, pulses, range_bins + LANES), jnp.float32),
            pltpu.VMEM((leaves, LANES), jnp.int32),
            pltpu.VMEM((leaves, LANES), jnp.float32),
            pltpu.VMEM((leaves, LANES), jnp.float32),
            pltpu.VMEM((2, pulses, LANES), jnp.float32),
            pltpu.VMEM((2, ap_count, range_bins // LANES, tile_rows, LANES), jnp.bfloat16),
            pltpu.VMEM((2, ap_count, range_bins // LANES, tile_rows, LANES), jnp.bfloat16),
            pltpu.VMEM((devices, tile_rows, tile_bins), jnp.bfloat16),
            pltpu.VMEM((2, devices, tile_rows, tile_bins), jnp.bfloat16),
            pltpu.VMEM((devices, tile_rows, tile_bins), jnp.bfloat16),
            pltpu.VMEM((devices, tile_rows, tile_bins), jnp.bfloat16),
            pltpu.VMEM((2, LANES), jnp.int32),
            pltpu.SMEM((2, LANES), jnp.int32),
            pltpu.SemaphoreType.DMA((2, 3)),
            pltpu.SemaphoreType.DMA((2, 3)),
            pltpu.SemaphoreType.DMA((2,)),
            pltpu.SemaphoreType.DMA((2,)),
            pltpu.SemaphoreType.DMA((2,)),
            pltpu.SemaphoreType.DMA((2,)),
            pltpu.SemaphoreType.DMA,
            pltpu.SemaphoreType.DMA((5,)),
        ],
        compiler_params=pltpu.CompilerParams(collective_id=0, has_side_effects=True, vmem_limit_bytes=24 * 2**20),
    )(
        *(
            pltpu.with_memory_space_constraint(operand, pltpu.HBM)
            for operand in (chirp, raw_echoes, range_offsets, phases, tile_table.T)
        )
    )
    return placed


def solution(mesh):
    placed = (P(None, "ap", "rg"), P(), P(None, None, "rg"), P(None, None, "rg"), P())
    return jax.shard_map(
        per_device, mesh=mesh, in_specs=placed, out_specs=P(None, "ap", "rg"), check_vma=False
    )
```
